256 devices in a mesh: dp: 8 (over z), context: 32 (over y, x, core).
Axes of the slice: x: 4, y: 4, z: 8, core: 2. Of those that a mesh axis runs over, the one named last changes fastest.
Arguments:
- query_in: bfloat16 [8, 16384, 1024], P('dp', 'context'), may hold values from -6 to 6
- key_in: bfloat16 [8, 16384, 1024], P('dp', 'context'), may hold values from -6 to 6
- value_in: bfloat16 [8, 16384, 1024], P('dp', 'context'), may hold values from -6 to 6
- out_grad: bfloat16 [8, 16384, 2048], P('dp', 'context'), may hold values from -6 to 6
- out_weight: bfloat16 [1024, 2048], P('context'), may hold values from -0.1875 to 0.1875
Outputs:
- output: bfloat16 [8, 16384, 2048], P('dp', 'context')
- query_grad: bfloat16 [8, 16384, 1024], P('dp', 'context')
- key_grad: bfloat16 [8, 16384, 1024], P('dp', 'context')
- value_grad: bfloat16 [8, 16384, 1024], P('dp', 'context')
- weight_grad: float32 [1024, 2048], P('context')
The draws below stay inside these ranges and needn't reach their ends.
All inputs are finite; a program needn't handle non-finite values.
Results may differ from the reference program's by a relative error of at most 0.025.
Values may be sent and summed in bfloat16 or wider, within the bound.
No kernel may reach another device: no remote copies, remote signals or barrier semaphores. Data moves between devices by JAX's collectives and lax.ppermute only.
A program may use at most 192 MiB of HBM per device.

```python
import math
import jax
import jax.numpy as jnp
from jax import lax

HEADS = 8
HEAD_DIM = 128
D = 2048
TOK_DEV = 512
HD = 1024
LENGTH = 16384
SEQS = 8


def steps_of(own_key, shape, shards, least, high):
    def one(position, shards_of):
        steps = jax.random.uniform(jax.random.fold_in(jax.random.fold_in(own_key, 6), position), (shards_of,), jnp.float32, least / len(shards), high / len(shards))
        return jnp.repeat(jnp.exp(steps), shape[position] // shards_of).reshape((-1,) + (1,) * (len(shape) - position - 1))

    gain = one(*shards[0])
    for cut in shards[1:]:
        gain = gain * one(*cut)
    return gain


def centred(own_key, shape, deviation, reach, split=(), held_as=jnp.bfloat16):
    factor_of = steps_of(own_key, shape, split, -0.22, 0.18) if split else 1.0
    entries = jax.random.normal(own_key, shape, jnp.float32) * deviation * factor_of
    return jnp.minimum(jnp.maximum(entries, -reach), reach).astype(held_as)


def setup_inputs(seed: int = 0) -> dict:
    splits = jax.random.split(jax.random.key(seed), 6)
    return {
        "query_in": centred(splits[0], (SEQS, LENGTH, HD), 1.0, 6.0, ((0, 8), (1, 32))),
        "key_in": centred(splits[1], (SEQS, LENGTH, HD), 1.0, 6.0, ((0, 8), (1, 32))),
        "value_in": centred(splits[2], (SEQS, LENGTH, HD), 1.0, 6.0, ((0, 8), (1, 32))),
        "out_grad": centred(splits[3], (SEQS, LENGTH, D), 1.0, 6.0, ((0, 8), (1, 32))),
        "out_weight": centred(splits[4], (HD, D), HD ** -0.5, 0.1875, ((0, 32),)),
    }


def to_blocks(array, seq_count, blocks):
    return array.reshape(seq_count * blocks, TOK_DEV, HEADS, HEAD_DIM)

def block_states(pieces):
    query_part, key_part, value_part, grad_part = pieces
    kv_part = jnp.einsum('shd,she->hde', key_part.astype(jnp.float32), value_part.astype(jnp.float32))
    qg_part = jnp.einsum('thd,the->hde', query_part.astype(jnp.float32), grad_part.astype(jnp.float32))
    return (kv_part, qg_part)

def reference(query_in, key_in, value_in, out_grad, out_weight):
    seq_count = query_in.shape[0]
    length = query_in.shape[1]
    head_width = query_in.shape[2]
    blocks = length // TOK_DEV
    att_scale = 1.0 / math.sqrt(HEAD_DIM * length)
    grad_scale = 1.0 / math.sqrt(seq_count * length)
    grad_flat = out_grad.reshape(seq_count * length, D)
    head_grad = jnp.dot(grad_flat, out_weight.T, preferred_element_type=jnp.float32).astype(jnp.bfloat16)
    query_blk = to_blocks(query_in, seq_count, blocks)
    key_blk = to_blocks(key_in, seq_count, blocks)
    value_blk = to_blocks(value_in, seq_count, blocks)
    grad_blk = to_blocks(head_grad, seq_count, blocks)
    kv_block, qg_block = lax.map(block_states, (query_blk, key_blk, value_blk, grad_blk))
    state_shape = (seq_count, blocks, HEADS, HEAD_DIM, HEAD_DIM)
    kv_block = kv_block.reshape(state_shape)
    qg_block = qg_block.reshape(state_shape)
    kv_incl = jnp.cumsum(kv_block, axis=1)
    kv_before = jnp.concatenate([jnp.zeros_like(kv_incl[:, :1]), kv_incl[:, :-1]], axis=1).astype(jnp.bfloat16)
    qg_incl = jnp.flip(jnp.cumsum(jnp.flip(qg_block, 1), axis=1), 1)
    qg_after = jnp.concatenate([qg_incl[:, 1:], jnp.zeros_like(qg_incl[:, :1])], axis=1).astype(jnp.bfloat16)
    kv_before = kv_before.reshape(seq_count * blocks, HEADS, HEAD_DIM, HEAD_DIM)
    qg_after = qg_after.reshape(seq_count * blocks, HEADS, HEAD_DIM, HEAD_DIM)
    positions = lax.broadcasted_iota(jnp.int32, (TOK_DEV, TOK_DEV), 0)
    sources = lax.broadcasted_iota(jnp.int32, (TOK_DEV, TOK_DEV), 1)
    causal = (positions >= sources)[None]

    def one_block(pieces):
        query_part, key_part, value_part, grad_part, kv_part, qg_part = pieces
        query_wide = query_part.astype(jnp.float32)
        key_wide = key_part.astype(jnp.float32)
        value_wide = value_part.astype(jnp.float32)
        grad_wide = grad_part.astype(jnp.float32)
        kv_wide = kv_part.astype(jnp.float32)
        qg_wide = qg_part.astype(jnp.float32)
        scores = jnp.einsum('thd,shd->hts', query_wide, key_wide) * att_scale
        scores = jnp.where(causal, scores, 0.0).astype(jnp.bfloat16).astype(jnp.float32)
        attended = jnp.einsum('hts,shd->thd', scores, value_wide) + att_scale * jnp.einsum('thd,hde->the', query_wide, kv_wide)
        back_scores = jnp.einsum('the,she->hts', grad_wide, value_wide) * att_scale
        back_scores = jnp.where(causal, back_scores, 0.0).astype(jnp.bfloat16).astype(jnp.float32)
        query_grad = jnp.einsum('hts,shd->thd', back_scores, key_wide) + att_scale * jnp.einsum('the,hde->thd', grad_wide, kv_wide)
        key_grad = jnp.einsum('hts,thd->shd', back_scores, query_wide) + att_scale * jnp.einsum('she,hde->shd', value_wide, qg_wide)
        value_grad = jnp.einsum('hts,the->she', scores, grad_wide) + att_scale * jnp.einsum('shd,hde->she', key_wide, qg_wide)
        return (attended.astype(jnp.bfloat16), query_grad.astype(jnp.bfloat16), key_grad.astype(jnp.bfloat16), value_grad.astype(jnp.bfloat16))
    attended, query_grad, key_grad, value_grad = lax.map(one_block, (query_blk, key_blk, value_blk, grad_blk, kv_before, qg_after))
    out_shape = (seq_count, length, head_width)
    attended_flat = attended.reshape(seq_count * length, head_width)
    output = jnp.dot(attended_flat, out_weight, preferred_element_type=jnp.float32).astype(jnp.bfloat16)
    weight_grad = jnp.dot(attended_flat.T, grad_flat, preferred_element_type=jnp.float32) * grad_scale
    return (output.reshape(seq_count, length, D), query_grad.reshape(out_shape), key_grad.reshape(out_shape), value_grad.reshape(out_shape), weight_grad)
```

```python
import math

import jax
import jax.numpy as jnp
from jax import lax
from jax.experimental import pallas as pl
from jax.experimental.pallas import tpu as pltpu
from jax.sharding import Mesh
from jax.sharding import PartitionSpec as P

HEADS = 8
HEAD_DIM = 128
BF16 = jnp.bfloat16
F32 = jnp.float32
CONTEXT = ("y", "x", "core")
PLANE = ("y", "x")
VMEM_BYTES = 56 * 1024 * 1024


def params():
    return pltpu.CompilerParams(vmem_limit_bytes=VMEM_BYTES)


def mul(a, b, a_dim, b_dim):
    return lax.dot_general(
        a, b, (((a_dim,), (b_dim,)), ((), ())), preferred_element_type=F32
    )


def kv_kernel(k_ref, v_ref, out_ref):
    out_ref[...] = mul(k_ref[...], v_ref[...], 0, 0).astype(BF16)


def kv_states(keys, values):
    toks, width = keys.shape
    return pl.pallas_call(
        kv_kernel,
        grid=(HEADS,),
        in_specs=[pl.BlockSpec((toks, HEAD_DIM), lambda h: (0, h))] * 2,
        out_specs=pl.BlockSpec((HEAD_DIM, HEAD_DIM), lambda h: (h, 0)),
        out_shape=jax.ShapeDtypeStruct((width, HEAD_DIM), BF16),
        compiler_params=params(),
        name="kv_states",
    )(keys, values)


def strict_prefix(pieces, backward):
    count = pieces.shape[0]

    def kernel(x_ref, out_ref):
        total = jnp.zeros(x_ref.shape[1:], F32)
        for step in range(count):
            at = count - 1 - step if backward else step
            out_ref[at] = total.astype(BF16)
            total = total + x_ref[at].astype(F32)

    return pl.pallas_call(
        kernel,
        out_shape=jax.ShapeDtypeStruct(pieces.shape, BF16),
        compiler_params=params(),
        name="strict_prefix",
    )(pieces)


def scan_states(states, backward):
    count = 32
    sent = states.reshape(count, states.shape[0] // count, HEAD_DIM)
    pieces = lax.all_to_all(sent, CONTEXT, 0, 0)
    prefixes = strict_prefix(pieces, backward)
    return lax.all_to_all(prefixes, CONTEXT, 0, 0).reshape(states.shape)


def causal_mask(rows):
    later = lax.broadcasted_iota(jnp.int32, (rows, rows), 0)
    earlier = lax.broadcasted_iota(jnp.int32, (rows, rows), 1)
    return later >= earlier


def attended_states(queries, keys, values, kv_before, att_scale):
    toks, width = queries.shape
    half = toks // 2

    def kernel(q_ref, k_ref, v_ref, s_ref, out_ref):
        mask = causal_mask(half)
        q0, q1 = q_ref[:half], q_ref[half:]
        k0, k1 = k_ref[:half], k_ref[half:]
        v0, v1 = v_ref[:half], v_ref[half:]
        state = s_ref[...]
        s00 = jnp.where(mask, mul(q0, k0, 1, 1) * att_scale, 0.0).astype(BF16)
        s10 = (mul(q1, k0, 1, 1) * att_scale).astype(BF16)
        s11 = jnp.where(mask, mul(q1, k1, 1, 1) * att_scale, 0.0).astype(BF16)
        out_ref[:half] = (mul(s00, v0, 1, 0) + att_scale * mul(q0, state, 1, 0)).astype(BF16)
        out_ref[half:] = (
            mul(s10, v0, 1, 0) + mul(s11, v1, 1, 0) + att_scale * mul(q1, state, 1, 0)
        ).astype(BF16)

    column = pl.BlockSpec((toks, HEAD_DIM), lambda h: (0, h))
    return pl.pallas_call(
        kernel,
        grid=(HEADS,),
        in_specs=[column] * 3 + [pl.BlockSpec((HEAD_DIM, HEAD_DIM), lambda h: (h, 0))],
        out_specs=column,
        out_shape=jax.ShapeDtypeStruct((toks, width), BF16),
        compiler_params=params(),
        name="attended",
    )(queries, keys, values, kv_before)


def pair_weight_grad(core, attended, attended_mate, grad, grad_mate, grad_scale):
    toks, width = attended.shape
    half = grad.shape[1] // 2
    rows = 256

    def kernel(core_ref, a_ref, am_ref, g_ref, gm_ref, out_ref):
        total = mul(a_ref[...], g_ref[...], 0, 0) + mul(am_ref[...], gm_ref[...], 0, 0)
        out_ref[...] = (total * grad_scale).astype(BF16)

    column = pl.BlockSpec((toks, rows), lambda i, c: (0, i))
    return pl.pallas_call(
        kernel,
        grid_spec=pltpu.PrefetchScalarGridSpec(
            num_scalar_prefetch=1,
            grid=(width // rows,),
            in_specs=[
                column,
                column,
                pl.BlockSpec((toks, half), lambda i, c: (0, c[0])),
                pl.BlockSpec((toks, half), lambda i, c: (0, 0)),
            ],
            out_specs=pl.BlockSpec((rows, half), lambda i, c: (i, 0)),
        ),
        out_shape=jax.ShapeDtypeStruct((width, half), BF16),
        compiler_params=params(),
        name="pair_weight_grad",
    )(core, attended, attended_mate, grad, grad_mate)


def sum_plane(pieces):
    count, rows, width = pieces.shape
    keep = rows // 2
    slices = width // HEAD_DIM

    def kernel(x_ref, out_ref):
        for part in range(slices):
            lanes = slice(part * HEAD_DIM, (part + 1) * HEAD_DIM)
            total = x_ref[0, :, lanes].astype(F32)
            for at in range(1, count):
                total = total + x_ref[at, :, lanes].astype(F32)
            total = total.astype(BF16)
            out_ref[part, 0] = total[:keep]
            out_ref[part, 1] = total[keep:]

    return pl.pallas_call(
        kernel,
        out_shape=jax.ShapeDtypeStruct((slices, 2, keep, HEAD_DIM), BF16),
        compiler_params=params(),
        name="sum_plane",
    )(pieces)


def sum_groups(pieces):
    count = pieces.shape[0]

    def kernel(x_ref, out_ref):
        total = x_ref[0].astype(F32)
        for at in range(1, count):
            total = total + x_ref[at].astype(F32)
        total = total.astype(BF16)
        for at in range(count):
            out_ref[at] = total

    return pl.pallas_call(
        kernel,
        out_shape=jax.ShapeDtypeStruct(pieces.shape, BF16),
        compiler_params=params(),
        name="sum_groups",
    )(pieces)


def lay_rows(pieces):
    slices, halves, rows, lanes = pieces.shape

    def kernel(x_ref, out_ref):
        for half in range(halves):
            for part in range(slices):
                start = (half * slices + part) * lanes
                out_ref[:, start : start + lanes] = x_ref[part, half].astype(F32)

    return pl.pallas_call(
        kernel,
        out_shape=jax.ShapeDtypeStruct((rows, halves * slices * lanes), F32),
        compiler_params=params(),
        name="lay_rows",
    )(pieces)


def head_grads(grad, weight, queries):
    toks, model = grad.shape
    width = weight.shape[0]
    rows = 256

    def kernel(g_ref, w_ref, q_ref, hg_ref, qg_ref):
        head_grad = mul(g_ref[...], w_ref[...], 1, 1).astype(BF16)
        hg_ref[...] = head_grad
        for h in range(rows // HEAD_DIM):
            lanes = slice(h * HEAD_DIM, (h + 1) * HEAD_DIM)
            qg_ref[lanes, :] = mul(q_ref[:, lanes], head_grad[:, lanes], 0, 0).astype(BF16)

    column = pl.BlockSpec((toks, rows), lambda i: (0, i))
    return pl.pallas_call(
        kernel,
        grid=(width // rows,),
        in_specs=[
            pl.BlockSpec((toks, model), lambda i: (0, 0)),
            pl.BlockSpec((rows, model), lambda i: (i, 0)),
            column,
        ],
        out_specs=[column, pl.BlockSpec((rows, HEAD_DIM), lambda i: (i, 0))],
        out_shape=[
            jax.ShapeDtypeStruct((toks, width), BF16),
            jax.ShapeDtypeStruct((width, HEAD_DIM), BF16),
        ],
        compiler_params=params(),
        name="head_grads",
    )(grad, weight, queries)


def project(attended, weight):
    toks, width = attended.shape
    model = weight.shape[1]
    columns = 512

    def kernel(a_ref, w_ref, out_ref):
        out_ref[...] = mul(a_ref[...], w_ref[...], 1, 0).astype(BF16)

    return pl.pallas_call(
        kernel,
        grid=(model // columns,),
        in_specs=[
            pl.BlockSpec((toks, width), lambda i: (0, 0)),
            pl.BlockSpec((width, columns), lambda i: (0, i)),
        ],
        out_specs=pl.BlockSpec((toks, columns), lambda i: (0, i)),
        out_shape=jax.ShapeDtypeStruct((toks, model), BF16),
        compiler_params=params(),
        name="project",
    )(attended, weight)


def input_grads(queries, keys, values, head_grad, kv_before, qg_after, att_scale):
    toks, width = queries.shape
    half = toks // 2

    def kernel(q_ref, k_ref, v_ref, g_ref, kv_ref, qg_ref, dq_ref, dk_ref, dv_ref):
        mask = causal_mask(half)
        q0, q1 = q_ref[:half], q_ref[half:]
        k0, k1 = k_ref[:half], k_ref[half:]
        v0, v1 = v_ref[:half], v_ref[half:]
        g0, g1 = g_ref[:half], g_ref[half:]
        kv, qg = kv_ref[...], qg_ref[...]
        s00 = jnp.where(mask, mul(q0, k0, 1, 1) * att_scale, 0.0).astype(BF16)
        s10 = (mul(q1, k0, 1, 1) * att_scale).astype(BF16)
        s11 = jnp.where(mask, mul(q1, k1, 1, 1) * att_scale, 0.0).astype(BF16)
        dv_ref[:half] = (
            mul(s00, g0, 0, 0) + mul(s10, g1, 0, 0) + att_scale * mul(k0, qg, 1, 0)
        ).astype(BF16)
        dv_ref[half:] = (mul(s11, g1, 0, 0) + att_scale * mul(k1, qg, 1, 0)).astype(BF16)
        b00 = jnp.where(mask, mul(g0, v0, 1, 1) * att_scale, 0.0).astype(BF16)
        b10 = (mul(g1, v0, 1, 1) * att_scale).astype(BF16)
        b11 = jnp.where(mask, mul(g1, v1, 1, 1) * att_scale, 0.0).astype(BF16)
        dq_ref[:half] = (mul(b00, k0, 1, 0) + att_scale * mul(g0, kv, 1, 1)).astype(BF16)
        dq_ref[half:] = (
            mul(b10, k0, 1, 0) + mul(b11, k1, 1, 0) + att_scale * mul(g1, kv, 1, 1)
        ).astype(BF16)
        dk_ref[:half] = (
            mul(b00, q0, 0, 0) + mul(b10, q1, 0, 0) + att_scale * mul(v0, qg, 1, 1)
        ).astype(BF16)
        dk_ref[half:] = (mul(b11, q1, 0, 0) + att_scale * mul(v1, qg, 1, 1)).astype(BF16)

    column = pl.BlockSpec((toks, HEAD_DIM), lambda h: (0, h))
    state = pl.BlockSpec((HEAD_DIM, HEAD_DIM), lambda h: (h, 0))
    return pl.pallas_call(
        kernel,
        grid=(HEADS,),
        in_specs=[column] * 4 + [state] * 2,
        out_specs=[column] * 3,
        out_shape=[jax.ShapeDtypeStruct((toks, width), BF16)] * 3,
        compiler_params=params(),
        name="input_grads",
    )(queries, keys, values, head_grad, kv_before, qg_after)


def swap_cores(value):
    return lax.ppermute(value, "core", [(0, 1), (1, 0)])


def on_device(query_in, key_in, value_in, out_grad, out_weight):
    queries, keys, values, grad = query_in[0], key_in[0], value_in[0], out_grad[0]
    toks = queries.shape[0]
    length = toks * 32
    att_scale = 1.0 / math.sqrt(HEAD_DIM * length)
    grad_scale = 1.0 / math.sqrt(length * 8)
    core = lax.axis_index("core")
    half = grad.shape[1] // 2

    weight = lax.all_gather(out_weight, CONTEXT, axis=0, tiled=True)
    grad_mate = swap_cores(lax.dynamic_slice_in_dim(grad, (1 - core) * half, half, 1))

    kv_before = scan_states(kv_states(keys, values), False)
    attended = attended_states(queries, keys, values, kv_before, att_scale)
    attended_mate = swap_cores(attended)
    terms = pair_weight_grad(
        jnp.reshape(core, (1,)), attended, attended_mate, grad, grad_mate, grad_scale
    )
    terms = lax.all_to_all(terms.reshape(16, 64, half), PLANE, 0, 0)
    plane_sum = sum_plane(terms).reshape(16, 32, HEAD_DIM)
    group_terms = lax.all_to_all(plane_sum, ("z", "core"), 0, 0)
    group_sum = sum_groups(group_terms.reshape(8, 2, 32, HEAD_DIM))
    weight_grad = lay_rows(lax.all_to_all(group_sum, "z", 0, 0))

    head_grad, qg_block = head_grads(grad, weight, queries)
    qg_after = scan_states(qg_block, True)
    output = project(attended, weight)
    query_grad, key_grad, value_grad = input_grads(
        queries, keys, values, head_grad, kv_before, qg_after, att_scale
    )
    return (output[None], query_grad[None], key_grad[None], value_grad[None], weight_grad)


def solution(mesh):
    fine = Mesh(mesh.devices.reshape(8, 4, 4, 2), ("z", "y", "x", "core"))
    rows = P("z", CONTEXT, None)
    owned = P(CONTEXT, None)
    return jax.shard_map(
        on_device,
        mesh=fine,
        in_specs=(rows, rows, rows, rows, owned),
        out_specs=(rows, rows, rows, rows, owned),
        check_vma=False,
    )
```

```python
import math

import jax
import jax.numpy as jnp
from jax import lax
from jax.experimental import pallas as pl
from jax.experimental.pallas import tpu as pltpu
from jax.sharding import Mesh
from jax.sharding import PartitionSpec as P

HEADS = 8
HEAD_DIM = 128
BF16 = jnp.bfloat16
F32 = jnp.float32
CONTEXT = ("y", "x", "core")
PLANE = ("y", "x")
WHOLE = pl.BlockSpec(memory_space=pltpu.VMEM)


def params(mib=16):
    return pltpu.CompilerParams(vmem_limit_bytes=mib * 1024 * 1024)


def in_hbm(value):
    return pltpu.with_memory_space_constraint(value, pltpu.HBM)


def mul(a, b, a_dim, b_dim):
    return lax.dot_general(
        a, b, (((a_dim,), (b_dim,)), ((), ())), preferred_element_type=F32
    )


def kv_states(keys, values):
    toks, width = keys.shape
    wide = 2 * HEAD_DIM

    def kernel(k_ref, v_ref, out_ref):
        both = mul(k_ref[...], v_ref[...], 0, 0)
        out_ref[:HEAD_DIM] = both[:HEAD_DIM, :HEAD_DIM].astype(BF16)
        out_ref[HEAD_DIM:] = both[HEAD_DIM:, HEAD_DIM:].astype(BF16)

    return pl.pallas_call(
        kernel,
        grid=(width // wide,),
        in_specs=[pl.BlockSpec((toks, wide), lambda h: (0, h))] * 2,
        out_specs=pl.BlockSpec((wide, HEAD_DIM), lambda h: (h, 0)),
        out_shape=pltpu.HBM((width, HEAD_DIM), BF16),
        compiler_params=params(),
        name="kv_states",
    )(in_hbm(keys), in_hbm(values))


def strict_prefix(pieces, backward):
    count = pieces.shape[0]

    def kernel(x_ref, out_ref):
        total = jnp.zeros(x_ref.shape[1:], F32)
        for step in range(count):
            at = count - 1 - step if backward else step
            out_ref[at] = total.astype(BF16)
            total = total + x_ref[at].astype(F32)

    return pl.pallas_call(
        kernel,
        out_shape=jax.ShapeDtypeStruct(pieces.shape, BF16),
        in_specs=[WHOLE],
        out_specs=WHOLE,
        compiler_params=params(4),
        name="strict_prefix",
    )(pieces)


def causal_mask(rows):
    later = lax.broadcasted_iota(jnp.int32, (rows, rows), 0)
    earlier = lax.broadcasted_iota(jnp.int32, (rows, rows), 1)
    return later >= earlier


def attended_states(queries, keys, values, kv_before, att_scale):
    toks, width = queries.shape
    half = toks // 2

    def kernel(q_ref, k_ref, v_ref, s_ref, out_ref):
        mask = causal_mask(half)
        q0, q1 = q_ref[:half], q_ref[half:]
        k0, k1 = k_ref[:half], k_ref[half:]
        v0, v1 = v_ref[:half], v_ref[half:]
        state = s_ref[...]
        s00 = jnp.where(mask, mul(q0, k0, 1, 1) * att_scale, 0.0).astype(BF16)
        s10 = (mul(q1, k0, 1, 1) * att_scale).astype(BF16)
        s11 = jnp.where(mask, mul(q1, k1, 1, 1) * att_scale, 0.0).astype(BF16)
        out_ref[:half] = (mul(s00, v0, 1, 0) + att_scale * mul(q0, state, 1, 0)).astype(BF16)
        out_ref[half:] = (
            mul(s10, v0, 1, 0) + mul(s11, v1, 1, 0) + att_scale * mul(q1, state, 1, 0)
        ).astype(BF16)

    column = pl.BlockSpec((toks, HEAD_DIM), lambda h: (0, h))
    return pl.pallas_call(
        kernel,
        grid=(HEADS,),
        in_specs=[column] * 3 + [pl.BlockSpec((HEAD_DIM, HEAD_DIM), lambda h: (h, 0))],
        out_specs=column,
        out_shape=pltpu.HBM((toks, width), BF16),
        compiler_params=params(),
        name="attended",
    )(in_hbm(queries), in_hbm(keys), in_hbm(values), kv_before)


def pair_weight_grad(core, attended, attended_mate, grad, grad_mate, grad_scale):
    toks, width = attended.shape
    half = grad.shape[1] // 2
    rows = 256

    def kernel(core_ref, a_ref, am_ref, g_ref, gm_ref, out_ref):
        total = mul(a_ref[...], g_ref[...], 0, 0) + mul(am_ref[...], gm_ref[...], 0, 0)
        out_ref[...] = (total * grad_scale).astype(BF16)

    column = pl.BlockSpec((toks, rows), lambda i, c: (0, i))
    return pl.pallas_call(
        kernel,
        grid_spec=pltpu.PrefetchScalarGridSpec(
            num_scalar_prefetch=1,
            grid=(width // rows,),
            in_specs=[
                column,
                column,
                pl.BlockSpec((toks, half), lambda i, c: (0, c[0])),
                pl.BlockSpec((toks, half), lambda i, c: (0, 0)),
            ],
            out_specs=pl.BlockSpec((rows, half), lambda i, c: (i, 0)),
        ),
        out_shape=pltpu.HBM((width, half), BF16),
        compiler_params=params(),
        name="pair_weight_grad",
    )(core, in_hbm(attended), attended_mate, in_hbm(grad), grad_mate)


def sum_plane(pieces):
    count, rows, width = pieces.shape
    keep = rows // 2
    slices = width // HEAD_DIM

    def kernel(x_ref, out_ref):
        for part in range(slices):
            lanes = slice(part * HEAD_DIM, (part + 1) * HEAD_DIM)
            total = x_ref[0, :, lanes].astype(F32)
            for at in range(1, count):
                total = total + x_ref[at, :, lanes].astype(F32)
            total = total.astype(BF16)
            out_ref[part, 0] = total[:keep]
            out_ref[part, 1] = total[keep:]

    return pl.pallas_call(
        kernel,
        out_shape=pltpu.HBM((slices, 2, keep, HEAD_DIM), BF16),
        in_specs=[WHOLE],
        out_specs=WHOLE,
        compiler_params=params(4),
        name="sum_plane",
    )(pieces)


def sum_groups(pieces):
    count = pieces.shape[0]

    def kernel(x_ref, out_ref):
        total = x_ref[0].astype(F32)
        for at in range(1, count):
            total = total + x_ref[at].astype(F32)
        total = total.astype(BF16)
        for at in range(count):
            out_ref[at] = total

    return pl.pallas_call(
        kernel,
        out_shape=pltpu.HBM(pieces.shape, BF16),
        in_specs=[WHOLE],
        out_specs=WHOLE,
        compiler_params=params(4),
        name="sum_groups",
    )(pieces)


def lay_rows(pieces):
    slices, halves, rows, lanes = pieces.shape

    def kernel(x_ref, out_ref):
        for half in range(halves):
            for part in range(slices):
                start = (half * slices + part) * lanes
                out_ref[:, start : start + lanes] = x_ref[part, half].astype(F32)

    return pl.pallas_call(
        kernel,
        out_shape=jax.ShapeDtypeStruct((rows, halves * slices * lanes), F32),
        in_specs=[WHOLE],
        out_specs=WHOLE,
        compiler_params=params(4),
        name="lay_rows",
    )(pieces)


def head_grads(core, grad, weight, queries):
    toks, model = grad.shape
    width = weight.shape[0]
    rows = 256
    steps = width // rows // 2

    def kernel(core_ref, g_ref, w_ref, q_ref, hg_ref, mine_ref, give_ref):
        head_grad = mul(g_ref[...], w_ref[...], 1, 1).astype(BF16)
        hg_ref[...] = head_grad
        step = pl.program_id(0)
        for h in range(rows // HEAD_DIM):
            lanes = slice(h * HEAD_DIM, (h + 1) * HEAD_DIM)
            state = mul(q_ref[:, lanes], head_grad[:, lanes], 0, 0).astype(BF16)
            at = pl.ds(pl.multiple_of((step % steps) * rows + h * HEAD_DIM, HEAD_DIM), HEAD_DIM)

            @pl.when(step // steps == core_ref[0])
            def _():
                mine_ref[at, :] = state

            @pl.when(step // steps != core_ref[0])
            def _():
                give_ref[at, :] = state

    column = pl.BlockSpec((toks, rows), lambda i, c: (0, i))
    return pl.pallas_call(
        kernel,
        grid_spec=pltpu.PrefetchScalarGridSpec(
            num_scalar_prefetch=1,
            grid=(width // rows,),
            in_specs=[
                pl.BlockSpec((toks, model), lambda i, c: (0, 0)),
                pl.BlockSpec((rows, model), lambda i, c: (i, 0)),
                column,
            ],
            out_specs=[column, WHOLE, WHOLE],
        ),
        out_shape=[
            pltpu.HBM((toks, width), BF16),
            jax.ShapeDtypeStruct((width // 2, HEAD_DIM), BF16),
            jax.ShapeDtypeStruct((width // 2, HEAD_DIM), BF16),
        ],
        compiler_params=params(20),
        name="head_grads",
    )(core, in_hbm(grad), in_hbm(weight), in_hbm(queries))


def chip_states(mine, mate):
    def kernel(a_ref, b_ref, out_ref):
        out_ref[...] = (a_ref[...].astype(F32) + b_ref[...].astype(F32)).astype(BF16)

    return pl.pallas_call(
        kernel,
        in_specs=[WHOLE] * 2,
        out_specs=WHOLE,
        out_shape=jax.ShapeDtypeStruct(mine.shape, BF16),
        compiler_params=params(4),
        name="chip_states",
    )(mine, mate)


def row_states(places, chip, pieces):
    def kernel(place_ref, chip_ref, a_ref, b_ref, c_ref, row_ref, later_ref):
        x = place_ref[1]
        total, later = chip_ref[...].astype(F32), jnp.zeros(chip_ref.shape, F32)
        for by, ref in enumerate((a_ref, b_ref, c_ref), 1):
            piece = ref[...].astype(F32)
            total = total + piece
            later = later + jnp.where(x + by < 4, piece, 0.0)
        row_ref[...] = total.astype(BF16)
        later_ref[...] = later

    return pl.pallas_call(
        kernel,
        in_specs=[pl.BlockSpec(memory_space=pltpu.SMEM)] + [WHOLE] * 4,
        out_specs=[WHOLE] * 2,
        out_shape=[jax.ShapeDtypeStruct(chip.shape, BF16), jax.ShapeDtypeStruct(chip.shape, F32)],
        compiler_params=params(4),
        name="row_states",
    )(places, chip, *pieces)


def final_states(places, later_here, mine, mate, pieces):
    def kernel(place_ref, later_ref, mine_ref, mate_ref, a_ref, b_ref, c_ref, keep_ref, give_ref):
        y, core = place_ref[0], place_ref[2]
        later = later_ref[...]
        for by, ref in enumerate((a_ref, b_ref, c_ref), 1):
            later = later + jnp.where(y + by < 4, ref[...].astype(F32), 0.0)
        second = jnp.where(core == 0, mate_ref[...], mine_ref[...]).astype(F32)
        first_core, second_core = later + second, later
        keep_ref[...] = jnp.where(core == 0, first_core, second_core).astype(BF16)
        give_ref[...] = jnp.where(core == 0, second_core, first_core).astype(BF16)

    return pl.pallas_call(
        kernel,
        in_specs=[pl.BlockSpec(memory_space=pltpu.SMEM)] + [WHOLE] * 6,
        out_specs=[WHOLE] * 2,
        out_shape=[jax.ShapeDtypeStruct(mine.shape, BF16)] * 2,
        compiler_params=params(4),
        name="final_states",
    )(places, later_here, mine, mate, *pieces)


def project(attended, weight):
    toks, width = attended.shape
    model = weight.shape[1]
    columns = 512

    def kernel(a_ref, w_ref, out_ref):
        out_ref[...] = mul(a_ref[...], w_ref[...], 1, 0).astype(BF16)

    return pl.pallas_call(
        kernel,
        grid=(model // columns,),
        in_specs=[
            pl.BlockSpec((toks, width), lambda i: (0, 0)),
            pl.BlockSpec((width, columns), lambda i: (0, i)),
        ],
        out_specs=pl.BlockSpec((toks, columns), lambda i: (0, i)),
        out_shape=pltpu.HBM((toks, model), BF16),
        compiler_params=params(),
        name="project",
    )(in_hbm(attended), in_hbm(weight))


def local_grads(queries, keys, values, head_grad, kv_before, att_scale):
    toks, width = queries.shape
    half = toks // 2

    def kernel(q_ref, k_ref, v_ref, g_ref, kv_ref, dq_ref, dk_ref, dv_ref):
        mask = causal_mask(half)
        q0, q1 = q_ref[:half], q_ref[half:]
        k0, k1 = k_ref[:half], k_ref[half:]
        v0, v1 = v_ref[:half], v_ref[half:]
        g0, g1 = g_ref[:half], g_ref[half:]
        kv = kv_ref[...]
        s00 = jnp.where(mask, mul(q0, k0, 1, 1) * att_scale, 0.0).astype(BF16)
        s10 = (mul(q1, k0, 1, 1) * att_scale).astype(BF16)
        s11 = jnp.where(mask, mul(q1, k1, 1, 1) * att_scale, 0.0).astype(BF16)
        dv_ref[:half] = mul(s00, g0, 0, 0) + mul(s10, g1, 0, 0)
        dv_ref[half:] = mul(s11, g1, 0, 0)
        b00 = jnp.where(mask, mul(g0, v0, 1, 1) * att_scale, 0.0).astype(BF16)
        b10 = (mul(g1, v0, 1, 1) * att_scale).astype(BF16)
        b11 = jnp.where(mask, mul(g1, v1, 1, 1) * att_scale, 0.0).astype(BF16)
        dq_ref[:half] = (mul(b00, k0, 1, 0) + att_scale * mul(g0, kv, 1, 1)).astype(BF16)
        dq_ref[half:] = (
            mul(b10, k0, 1, 0) + mul(b11, k1, 1, 0) + att_scale * mul(g1, kv, 1, 1)
        ).astype(BF16)
        dk_ref[:half] = mul(b00, q0, 0, 0) + mul(b10, q1, 0, 0)
        dk_ref[half:] = mul(b11, q1, 0, 0)

    column = pl.BlockSpec((toks, HEAD_DIM), lambda h: (0, h))
    state = pl.BlockSpec((HEAD_DIM, HEAD_DIM), lambda h: (h, 0))
    return pl.pallas_call(
        kernel,
        grid=(HEADS,),
        in_specs=[column] * 4 + [state],
        out_specs=[column] * 3,
        out_shape=[
            pltpu.HBM((toks, width), BF16),
            pltpu.HBM((toks, width), F32),
            pltpu.HBM((toks, width), F32),
        ],
        compiler_params=params(12),
        name="local_grads",
    )(in_hbm(queries), in_hbm(keys), in_hbm(values), in_hbm(head_grad), kv_before)


def later_grads(core, keys, values, key_local, value_local, keep, back, att_scale):
    toks, width = keys.shape
    rows = keep.shape[0]
    heads = rows // HEAD_DIM

    def kernel(core_ref, k_ref, v_ref, dkl_ref, dvl_ref, keep_ref, back_ref, dk_ref, dv_ref):
        mine = pl.program_id(0) // heads == core_ref[0]
        qg = jnp.where(mine, keep_ref[...], back_ref[...])
        dk_ref[...] = (dkl_ref[...] + att_scale * mul(v_ref[...], qg, 1, 1)).astype(BF16)
        dv_ref[...] = (dvl_ref[...] + att_scale * mul(k_ref[...], qg, 1, 0)).astype(BF16)

    column = pl.BlockSpec((toks, HEAD_DIM), lambda h, c: (0, h))
    state = pl.BlockSpec((HEAD_DIM, HEAD_DIM), lambda h, c: (h % heads, 0))
    return pl.pallas_call(
        kernel,
        grid_spec=pltpu.PrefetchScalarGridSpec(
            num_scalar_prefetch=1,
            grid=(HEADS,),
            in_specs=[column] * 4 + [state] * 2,
            out_specs=[column] * 2,
        ),
        out_shape=[pltpu.HBM((toks, width), BF16)] * 2,
        compiler_params=params(12),
        name="later_grads",
    )(core, in_hbm(keys), in_hbm(values), in_hbm(key_local), in_hbm(value_local), keep, back)


def swap_cores(value):
    return lax.ppermute(value, "core", [(0, 1), (1, 0)])


def turn(value, axis, count, by):
    return lax.ppermute(value, axis, [(at, (at + by) % count) for at in range(count)])


def after(value, *others):
    return lax.optimization_barrier((value,) + others)[0]


def around(value, axis, sign):
    return [turn(value, axis, 4, sign * by) for by in (1, 2, 3)]


def on_device(query_in, key_in, value_in, out_grad, out_weight):
    queries, keys, values, grad = query_in[0], key_in[0], value_in[0], out_grad[0]
    toks = queries.shape[0]
    length = toks * 32
    att_scale = 1.0 / math.sqrt(HEAD_DIM * length)
    grad_scale = 1.0 / math.sqrt(length * 8)
    core = lax.axis_index("core")
    half = grad.shape[1] // 2
    places = jnp.stack([lax.axis_index("y"), lax.axis_index("x"), core])
    core_place = jnp.reshape(core, (1,))

    grad_mate = swap_cores(lax.dynamic_slice_in_dim(grad, (1 - core) * half, half, 1))
    weight = lax.all_gather(out_weight, CONTEXT, axis=0, tiled=True)
    kv_block = kv_states(keys, values)

    pieces = lax.all_to_all(kv_block.reshape(32, -1, HEAD_DIM), CONTEXT, 0, 0)
    prefixes = strict_prefix(after(pieces, grad_mate), False)
    kv_before = lax.all_to_all(prefixes, CONTEXT, 0, 0).reshape(kv_block.shape)

    attended = attended_states(queries, keys, values, kv_before, att_scale)
    attended_mate = swap_cores(attended)
    terms = pair_weight_grad(core_place, attended, attended_mate, grad, grad_mate, grad_scale)
    plane_terms = lax.all_to_all(terms.reshape(16, 64, half), PLANE, 0, 0)

    head_grad, mine, give = head_grads(core_place, after(grad, terms), weight, queries)
    mate = swap_cores(give)
    chip = chip_states(mine, mate)
    row_state, later_here = row_states(places, chip, around(chip, "x", -1))
    query_grad, key_local, value_local = local_grads(
        queries, keys, values, head_grad, kv_before, att_scale
    )
    output = project(attended, weight)

    plane_terms = after(plane_terms, key_local, output, row_state)
    plane_sum = sum_plane(plane_terms)
    group_terms = lax.all_to_all(plane_sum.reshape(16, 32, HEAD_DIM), ("z", "core"), 0, 0)
    row_pieces = around(after(row_state, plane_sum), "y", -1)
    keep, give = final_states(places, later_here, mine, mate, row_pieces)
    back = swap_cores(give)
    group_sum = sum_groups(group_terms.reshape(8, 2, 32, HEAD_DIM))
    weight_grad = lay_rows(lax.all_to_all(group_sum, "z", 0, 0))

    key_grad, value_grad = later_grads(
        core_place, keys, values, key_local, value_local, after(keep, group_sum), back, att_scale
    )
    return (output[None], query_grad[None], key_grad[None], value_grad[None], weight_grad)


def solution(mesh):
    fine = Mesh(mesh.devices.reshape(8, 4, 4, 2), ("z", "y", "x", "core"))
    rows = P("z", CONTEXT, None)
    owned = P(CONTEXT, None)
    return jax.shard_map(
        on_device,
        mesh=fine,
        in_specs=(rows, rows, rows, rows, owned),
        out_specs=(rows, rows, rows, rows, owned),
        check_vma=False,
    )
```

```python
import math

import jax
import jax.numpy as jnp
from jax import lax
from jax.experimental import pallas as pl
from jax.experimental.pallas import tpu as pltpu
from jax.sharding import Mesh
from jax.sharding import PartitionSpec as P

HEADS = 8
HEAD_DIM = 128
BF16 = jnp.bfloat16
F32 = jnp.float32
CONTEXT = ("y", "x", "core")
PLANE = ("y", "x")
WHOLE = pl.BlockSpec(memory_space=pltpu.VMEM)
SCALARS = pl.BlockSpec(memory_space=pltpu.SMEM)
IN_PLACE = pl.BlockSpec(memory_space=pl.ANY)


def params(mib=16):
    return pltpu.CompilerParams(vmem_limit_bytes=mib * 1024 * 1024)


def in_hbm(value):
    return pltpu.with_memory_space_constraint(value, pltpu.HBM)


def mul(a, b, a_dim, b_dim):
    return lax.dot_general(
        a, b, (((a_dim,), (b_dim,)), ((), ())), preferred_element_type=F32
    )


def kv_states(keys, values):
    toks, width = keys.shape
    wide = 2 * HEAD_DIM
    parts = 2
    span = width // parts

    def kernel(k_ref, v_ref, out_ref, k_buf, v_buf, sems):
        copies = []
        for part in range(parts):
            lanes = slice(part * span, (part + 1) * span)
            for at, (src, dst) in enumerate(((k_ref, k_buf), (v_ref, v_buf))):
                copy = pltpu.make_async_copy(src.at[:, lanes], dst.at[:, lanes], sems.at[at, part])
                copy.start()
                copies.append(copy)
        for part in range(parts):
            copies[2 * part].wait()
            copies[2 * part + 1].wait()
            for start in range(part * span, (part + 1) * span, wide):
                both = mul(k_buf[:, start : start + wide], v_buf[:, start : start + wide], 0, 0)
                middle = start + HEAD_DIM
                out_ref[start:middle] = both[:HEAD_DIM, :HEAD_DIM].astype(BF16)
                out_ref[middle : start + wide] = both[HEAD_DIM:, HEAD_DIM:].astype(BF16)

    return pl.pallas_call(
        kernel,
        in_specs=[IN_PLACE] * 2,
        out_specs=WHOLE,
        out_shape=jax.ShapeDtypeStruct((width, HEAD_DIM), BF16),
        scratch_shapes=[pltpu.VMEM((toks, width), BF16)] * 2
        + [pltpu.SemaphoreType.DMA((2, parts))],
        compiler_params=params(8),
        name="kv_states",
    )(in_hbm(keys), in_hbm(values))


def strict_prefix(pieces, backward):
    count = pieces.shape[0]

    def kernel(x_ref, out_ref):
        total = jnp.zeros(x_ref.shape[1:], F32)
        for step in range(count):
            at = count - 1 - step if backward else step
            out_ref[at] = total.astype(BF16)
            total = total + x_ref[at].astype(F32)

    return pl.pallas_call(
        kernel,
        out_shape=jax.ShapeDtypeStruct(pieces.shape, BF16),
        in_specs=[WHOLE],
        out_specs=WHOLE,
        compiler_params=params(4),
        name="strict_prefix",
    )(pieces)


def causal_mask(rows):
    later = lax.broadcasted_iota(jnp.int32, (rows, rows), 0)
    earlier = lax.broadcasted_iota(jnp.int32, (rows, rows), 1)
    return later >= earlier


def head_lanes(head):
    return slice(head * HEAD_DIM, (head + 1) * HEAD_DIM)


def attended_states(queries, keys, values, kv_before, att_scale):
    toks, width = queries.shape
    half = toks // 2

    def kernel(q_ref, k_ref, v_ref, s_ref, out_ref):
        mask = causal_mask(half)
        for head in range(HEADS):
            lanes = head_lanes(head)
            q0, q1 = q_ref[:half, lanes], q_ref[half:, lanes]
            k0, k1 = k_ref[:half, lanes], k_ref[half:, lanes]
            v0, v1 = v_ref[:half, lanes], v_ref[half:, lanes]
            state = s_ref[lanes, :]
            s00 = jnp.where(mask, mul(q0, k0, 1, 1) * att_scale, 0.0).astype(BF16)
            s10 = (mul(q1, k0, 1, 1) * att_scale).astype(BF16)
            s11 = jnp.where(mask, mul(q1, k1, 1, 1) * att_scale, 0.0).astype(BF16)
            out_ref[:half, lanes] = (
                mul(s00, v0, 1, 0) + att_scale * mul(q0, state, 1, 0)
            ).astype(BF16)
            out_ref[half:, lanes] = (
                mul(s10, v0, 1, 0) + mul(s11, v1, 1, 0) + att_scale * mul(q1, state, 1, 0)
            ).astype(BF16)

    return pl.pallas_call(
        kernel,
        in_specs=[WHOLE] * 4,
        out_specs=WHOLE,
        out_shape=jax.ShapeDtypeStruct((toks, width), BF16),
        compiler_params=params(8),
        name="attended",
    )(queries, keys, values, kv_before)


def pair_weight_grad(core, attended, attended_mate, grad, grad_mate, grad_scale):
    width = attended.shape[1]
    half = grad.shape[1] // 2
    rows = 512

    def kernel(core_ref, a_ref, am_ref, g_ref, gm_ref, out_ref):
        features = pl.ds(pl.multiple_of(pl.program_id(0) * rows, rows), rows)
        columns = pl.ds(pl.multiple_of(core_ref[0] * half, half), half)
        total = mul(a_ref[:, features], g_ref[:, columns], 0, 0)
        total = total + mul(am_ref[:, features], gm_ref[:, columns], 0, 0)
        out_ref[...] = (total * grad_scale).astype(BF16)

    return pl.pallas_call(
        kernel,
        grid=(width // rows,),
        in_specs=[SCALARS] + [WHOLE] * 4,
        out_specs=pl.BlockSpec((rows, half), lambda i: (i, 0)),
        out_shape=pltpu.HBM((width, half), BF16),
        compiler_params=params(12),
        name="pair_weight_grad",
    )(core, attended, attended_mate, grad, grad_mate)


def sum_plane(pieces):
    count, rows, width = pieces.shape
    keep = rows // 2
    slices = width // HEAD_DIM

    def kernel(x_ref, out_ref):
        for part in range(slices):
            lanes = slice(part * HEAD_DIM, (part + 1) * HEAD_DIM)
            total = x_ref[0, :, lanes].astype(F32)
            for at in range(1, count):
                total = total + x_ref[at, :, lanes].astype(F32)
            total = total.astype(BF16)
            out_ref[part, 0] = total[:keep]
            out_ref[part, 1] = total[keep:]

    return pl.pallas_call(
        kernel,
        out_shape=pltpu.HBM((slices, 2, keep, HEAD_DIM), BF16),
        in_specs=[WHOLE],
        out_specs=WHOLE,
        compiler_params=params(4),
        name="sum_plane",
    )(pieces)


def sum_groups(pieces):
    count = pieces.shape[0]

    def kernel(x_ref, out_ref):
        total = x_ref[0].astype(F32)
        for at in range(1, count):
            total = total + x_ref[at].astype(F32)
        total = total.astype(BF16)
        for at in range(count):
            out_ref[at] = total

    return pl.pallas_call(
        kernel,
        out_shape=pltpu.HBM(pieces.shape, BF16),
        in_specs=[WHOLE],
        out_specs=WHOLE,
        compiler_params=params(4),
        name="sum_groups",
    )(pieces)


def lay_rows(pieces):
    slices, halves, rows, lanes = pieces.shape

    def kernel(x_ref, out_ref):
        for half in range(halves):
            for part in range(slices):
                start = (half * slices + part) * lanes
                out_ref[:, start : start + lanes] = x_ref[part, half].astype(F32)

    return pl.pallas_call(
        kernel,
        out_shape=jax.ShapeDtypeStruct((rows, halves * slices * lanes), F32),
        in_specs=[WHOLE],
        out_specs=WHOLE,
        compiler_params=params(4),
        name="lay_rows",
    )(pieces)


def join_row(places, own, others):
    def kernel(place_ref, own_ref, a_ref, b_ref, c_ref, out_ref):
        x = place_ref[1]
        for by, ref in enumerate((own_ref, a_ref, b_ref, c_ref)):
            out_ref[lax.rem(x - by + 4, 4)] = ref[...]

    return pl.pallas_call(
        kernel,
        in_specs=[SCALARS] + [WHOLE] * 4,
        out_specs=WHOLE,
        out_shape=jax.ShapeDtypeStruct((4, *own.shape), BF16),
        compiler_params=params(4),
        name="join_row",
    )(places, own, *others)


def head_grads(places, grad, queries, attended, mine_parts, mate_parts):
    toks, model = grad.shape
    width = queries.shape[1]
    piece = mine_parts[0].shape[1]
    rows = 8 * piece
    half = width // 2

    def kernel(place_ref, grad_ref, query_ref, a_ref, *refs):
        sides = refs[:4], refs[4:8]
        hg_ref, mine_ref, give_ref, out_ref, g_ref, q_ref, buf, grad_sem, query_sem, sems = refs[8:]
        grad_copy = pltpu.make_async_copy(grad_ref, g_ref, grad_sem)
        grad_copy.start()
        query_copy = pltpu.make_async_copy(query_ref, q_ref, query_sem)
        query_copy.start()
        y, core = place_ref[0], place_ref[2]
        blocks = [lax.rem(y - by + 4, 4) for by in range(4)]
        waits = []
        for by in range(4):
            group = []
            for side in range(2):
                owner = core if side == 0 else 1 - core
                target = buf.at[blocks[by], :, owner]
                group.append(pltpu.make_async_copy(sides[side][by], target, sems.at[by, side]))
            waits.append(group)
        order = (0, 1, 3, 2)
        for by in order:
            for copy in waits[by]:
                copy.start()
        grad_copy.wait()
        query_copy.wait()
        for by in order:
            for copy in waits[by]:
                copy.wait()
            lanes = pl.ds(pl.multiple_of(blocks[by] * rows, rows), rows)
            block = buf[blocks[by]].reshape(rows, model)
            middle = toks // 2
            head_grad = jnp.concatenate(
                [mul(g_ref[:middle], block, 1, 1), mul(g_ref[middle:], block, 1, 1)], 0
            ).astype(BF16)
            hg_ref[:, lanes] = head_grad
            query = q_ref[:, lanes]
            states = [
                mul(query[:, head_lanes(h)], head_grad[:, head_lanes(h)], 0, 0)
                for h in range(rows // HEAD_DIM)
            ]
            state = jnp.concatenate(states, 0).astype(BF16)
            place = pl.ds(pl.multiple_of(lax.rem(blocks[by], 2) * rows, rows), rows)
            here = blocks[by] // 2 == core

            @pl.when(here)
            def _():
                mine_ref[place, :] = state

            @pl.when(jnp.logical_not(here))
            def _():
                give_ref[place, :] = state

        for start in range(0, model, 512):
            columns = slice(start, start + 512)
            wide = buf[:, :, :, :, columns].reshape(width, 512)
            out_ref[:, columns] = mul(a_ref[...], wide, 1, 0).astype(BF16)

    return pl.pallas_call(
        kernel,
        in_specs=[SCALARS, IN_PLACE, IN_PLACE, WHOLE] + [IN_PLACE] * 8,
        out_specs=[WHOLE] * 4,
        out_shape=[
            jax.ShapeDtypeStruct((toks, width), BF16),
            jax.ShapeDtypeStruct((half, HEAD_DIM), BF16),
            jax.ShapeDtypeStruct((half, HEAD_DIM), BF16),
            jax.ShapeDtypeStruct((toks, model), BF16),
        ],
        scratch_shapes=[
            pltpu.VMEM((toks, model), BF16),
            pltpu.VMEM((toks, width), BF16),
            pltpu.VMEM((4, 4, 2, piece, model), BF16),
            pltpu.SemaphoreType.DMA,
            pltpu.SemaphoreType.DMA,
            pltpu.SemaphoreType.DMA((4, 2)),
        ],
        compiler_params=params(12),
        name="head_grads",
    )(places, in_hbm(grad), in_hbm(queries), attended, *[in_hbm(part) for part in (*mine_parts, *mate_parts)])


def chip_states(mine, mate):
    def kernel(a_ref, b_ref, out_ref):
        out_ref[...] = (a_ref[...].astype(F32) + b_ref[...].astype(F32)).astype(BF16)

    return pl.pallas_call(
        kernel,
        in_specs=[WHOLE] * 2,
        out_specs=WHOLE,
        out_shape=jax.ShapeDtypeStruct(mine.shape, BF16),
        compiler_params=params(4),
        name="chip_states",
    )(mine, mate)


def row_states(places, chip, pieces):
    def kernel(place_ref, chip_ref, a_ref, b_ref, c_ref, row_ref, later_ref):
        x = place_ref[1]
        total, later = chip_ref[...].astype(F32), jnp.zeros(chip_ref.shape, F32)
        for by, ref in enumerate((a_ref, b_ref, c_ref), 1):
            piece = ref[...].astype(F32)
            total = total + piece
            later = later + jnp.where(x + by < 4, piece, 0.0)
        row_ref[...] = total.astype(BF16)
        later_ref[...] = later

    return pl.pallas_call(
        kernel,
        in_specs=[pl.BlockSpec(memory_space=pltpu.SMEM)] + [WHOLE] * 4,
        out_specs=[WHOLE] * 2,
        out_shape=[jax.ShapeDtypeStruct(chip.shape, BF16), jax.ShapeDtypeStruct(chip.shape, F32)],
        compiler_params=params(4),
        name="row_states",
    )(places, chip, *pieces)


def final_states(places, later_here, mine, mate, pieces):
    def kernel(place_ref, later_ref, mine_ref, mate_ref, a_ref, b_ref, c_ref, keep_ref, give_ref):
        y, core = place_ref[0], place_ref[2]
        later = later_ref[...]
        for by, ref in enumerate((a_ref, b_ref, c_ref), 1):
            later = later + jnp.where(y + by < 4, ref[...].astype(F32), 0.0)
        second = jnp.where(core == 0, mate_ref[...], mine_ref[...]).astype(F32)
        first_core, second_core = later + second, later
        keep_ref[...] = jnp.where(core == 0, first_core, second_core).astype(BF16)
        give_ref[...] = jnp.where(core == 0, second_core, first_core).astype(BF16)

    return pl.pallas_call(
        kernel,
        in_specs=[pl.BlockSpec(memory_space=pltpu.SMEM)] + [WHOLE] * 6,
        out_specs=[WHOLE] * 2,
        out_shape=[jax.ShapeDtypeStruct(mine.shape, BF16)] * 2,
        compiler_params=params(4),
        name="final_states",
    )(places, later_here, mine, mate, *pieces)


def local_grads(queries, keys, values, head_grad, kv_before, att_scale):
    toks, width = queries.shape
    half = toks // 2
    group = HEADS // 2

    def kernel(q_ref, k_ref, v_ref, g_ref, kv_ref, dq_ref, dk_ref, dv_ref):
        positions = lax.broadcasted_iota(jnp.int32, (half, half), 0)
        sources = lax.broadcasted_iota(jnp.int32, (half, half), 1)
        causal, turned = positions >= sources, positions <= sources

        def scaled(left, right, mask=None):
            scores = mul(left, right, 1, 1) * att_scale
            return (scores if mask is None else jnp.where(mask, scores, 0.0)).astype(BF16)

        for head in range(group):
            first = (pl.program_id(0) * group + head) * HEAD_DIM
            lanes = pl.ds(pl.multiple_of(first, HEAD_DIM), HEAD_DIM)
            here = head_lanes(head)
            q0, q1 = q_ref[:half, lanes], q_ref[half:, lanes]
            k0, k1 = k_ref[:half, lanes], k_ref[half:, lanes]
            v0, v1 = v_ref[:half, lanes], v_ref[half:, lanes]
            g0, g1 = g_ref[:half, lanes], g_ref[half:, lanes]
            kv = kv_ref[lanes, :]
            dv_ref[:half, here] = mul(scaled(k0, q0, turned), g0, 1, 0) + mul(
                scaled(k0, q1), g1, 1, 0
            )
            dv_ref[half:, here] = mul(scaled(k1, q1, turned), g1, 1, 0)
            b00, b10, b11 = scaled(g0, v0, causal), scaled(g1, v0), scaled(g1, v1, causal)
            dk_ref[:half, here] = mul(b00, q0, 0, 0) + mul(b10, q1, 0, 0)
            dk_ref[half:, here] = mul(b11, q1, 0, 0)
            dq_ref[:half, here] = (mul(b00, k0, 1, 0) + att_scale * mul(g0, kv, 1, 1)).astype(BF16)
            dq_ref[half:, here] = (
                mul(b10, k0, 1, 0) + mul(b11, k1, 1, 0) + att_scale * mul(g1, kv, 1, 1)
            ).astype(BF16)

    return pl.pallas_call(
        kernel,
        grid=(HEADS // group,),
        in_specs=[WHOLE] * 5,
        out_specs=[pl.BlockSpec((toks, group * HEAD_DIM), lambda i: (0, i))] * 3,
        out_shape=[
            pltpu.HBM((toks, width), BF16),
            pltpu.HBM((toks, width), F32),
            pltpu.HBM((toks, width), F32),
        ],
        compiler_params=params(12),
        name="local_grads",
    )(queries, keys, values, head_grad, kv_before)


def later_grads(core, keys, values, key_local, value_local, keep, back, att_scale):
    toks, width = keys.shape
    heads = keep.shape[0] // HEAD_DIM
    rows = 128

    def kernel(core_ref, k_ref, v_ref, dkl_ref, dvl_ref, keep_ref, back_ref, dk_ref, dv_ref):
        here = pl.ds(pl.multiple_of(pl.program_id(0) * rows, rows), rows)
        for head in range(HEADS):
            lanes, state = head_lanes(head), head_lanes(head % heads)
            mine = core_ref[0] == head // heads
            qg = jnp.where(mine, keep_ref[state, :], back_ref[state, :])
            dk_ref[:, lanes] = (
                dkl_ref[:, lanes] + att_scale * mul(v_ref[here, lanes], qg, 1, 1)
            ).astype(BF16)
            dv_ref[:, lanes] = (
                dvl_ref[:, lanes] + att_scale * mul(k_ref[here, lanes], qg, 1, 0)
            ).astype(BF16)

    block = pl.BlockSpec((rows, width), lambda i: (i, 0))
    return pl.pallas_call(
        kernel,
        grid=(toks // rows,),
        in_specs=[SCALARS, WHOLE, WHOLE, block, block, WHOLE, WHOLE],
        out_specs=[block] * 2,
        out_shape=[pltpu.HBM((toks, width), BF16)] * 2,
        compiler_params=params(8),
        name="later_grads",
    )(core, keys, values, in_hbm(key_local), in_hbm(value_local), keep, back)


def swap_cores(value):
    return lax.ppermute(value, "core", [(0, 1), (1, 0)])


def turn(value, axis, count, by):
    return lax.ppermute(value, axis, [(at, (at + by) % count) for at in range(count)])


def after(value, *others):
    return lax.optimization_barrier((value,) + others)[0]


def around(value, axis, sign):
    return [turn(value, axis, 4, sign * by) for by in (1, 2, 3)]


def on_device(query_in, key_in, value_in, out_grad, out_weight):
    queries, keys, values, grad = query_in[0], key_in[0], value_in[0], out_grad[0]
    toks = queries.shape[0]
    length = toks * 32
    att_scale = 1.0 / math.sqrt(HEAD_DIM * length)
    grad_scale = 1.0 / math.sqrt(length * 8)
    core = lax.axis_index("core")
    half = grad.shape[1] // 2
    places = jnp.stack([lax.axis_index("y"), lax.axis_index("x"), core])
    core_place = jnp.reshape(core, (1,))

    shards = around(out_weight, "x", 1)
    far_shard = turn(out_weight, "y", 4, 2)
    grad_mate = swap_cores(grad)
    kv_block = kv_states(keys, values)

    pieces = lax.all_to_all(kv_block.reshape(32, -1, HEAD_DIM), CONTEXT, 0, 0)
    prefixes = strict_prefix(after(pieces, grad_mate, far_shard, *shards), False)
    row = join_row(places, after(out_weight, prefixes), shards)
    low, high = turn(row, "y", 4, 1), turn(row, "y", 4, -1)
    far_shard = after(far_shard, prefixes)
    far_shards = around(far_shard, "x", 1)
    kv_before = lax.all_to_all(prefixes, CONTEXT, 0, 0).reshape(kv_block.shape)

    far_row = join_row(places, far_shard, far_shards)
    kv_before = after(kv_before, low, high, far_row)
    attended = attended_states(queries, keys, values, kv_before, att_scale)
    attended_mate = swap_cores(attended)
    terms = pair_weight_grad(core_place, attended, attended_mate, grad, grad_mate, grad_scale)
    plane_terms = lax.all_to_all(terms.reshape(16, 64, half), PLANE, 0, 0)

    weight_mine = [row, low, far_row, high]
    weight_mate = [swap_cores(after(part, terms)) for part in weight_mine]
    head_grad, mine, give, output = head_grads(
        after(places, terms), grad, queries, attended, weight_mine, weight_mate
    )
    mate = swap_cores(give)
    chip = chip_states(mine, mate)
    row_state, later_here = row_states(places, chip, around(chip, "x", -1))
    query_grad, key_local, value_local = local_grads(
        queries, keys, values, head_grad, kv_before, att_scale
    )

    plane_terms = after(plane_terms, key_local, row_state)
    plane_sum = sum_plane(plane_terms)
    group_terms = lax.all_to_all(plane_sum.reshape(16, 32, HEAD_DIM), ("z", "core"), 0, 0)
    row_pieces = around(after(row_state, plane_sum), "y", -1)
    keep, give = final_states(places, later_here, mine, mate, row_pieces)
    back = swap_cores(give)
    group_sum = sum_groups(group_terms.reshape(8, 2, 32, HEAD_DIM))
    weight_grad = lay_rows(lax.all_to_all(group_sum, "z", 0, 0))

    key_grad, value_grad = later_grads(
        core_place, keys, values, key_local, value_local, after(keep, group_sum), back, att_scale
    )
    return (output[None], query_grad[None], key_grad[None], value_grad[None], weight_grad)


def solution(mesh):
    fine = Mesh(mesh.devices.reshape(8, 4, 4, 2), ("z", "y", "x", "core"))
    rows = P("z", CONTEXT, None)
    owned = P(CONTEXT, None)
    return jax.shard_map(
        on_device,
        mesh=fine,
        in_specs=(rows, rows, rows, rows, owned),
        out_specs=(rows, rows, rows, rows, owned),
        check_vma=False,
    )
```

```python
import math

import jax
import jax.numpy as jnp
from jax import lax
from jax.experimental import pallas as pl
from jax.experimental.pallas import tpu as pltpu
from jax.sharding import Mesh
from jax.sharding import PartitionSpec as P

HEADS = 8
HEAD_DIM = 128
BF16 = jnp.bfloat16
F32 = jnp.float32
CONTEXT = ("y", "x", "core")
PLANE = ("y", "x")
WHOLE = pl.BlockSpec(memory_space=pltpu.VMEM)
SCALARS = pl.BlockSpec(memory_space=pltpu.SMEM)
IN_PLACE = pl.BlockSpec(memory_space=pl.ANY)


def params(mib=16):
    return pltpu.CompilerParams(vmem_limit_bytes=mib * 1024 * 1024)


def in_hbm(value):
    return pltpu.with_memory_space_constraint(value, pltpu.HBM)


def mul(a, b, a_dim, b_dim):
    return lax.dot_general(
        a, b, (((a_dim,), (b_dim,)), ((), ())), preferred_element_type=F32
    )


def kv_states(keys, values):
    toks, width = keys.shape
    wide = 2 * HEAD_DIM
    parts = 2
    span = width // parts

    def kernel(k_ref, v_ref, out_ref, k_buf, v_buf, sems):
        copies = []
        for part in range(parts):
            lanes = slice(part * span, (part + 1) * span)
            for at, (src, dst) in enumerate(((k_ref, k_buf), (v_ref, v_buf))):
                copy = pltpu.make_async_copy(src.at[:, lanes], dst.at[:, lanes], sems.at[at, part])
                copy.start()
                copies.append(copy)
        for part in range(parts):
            copies[2 * part].wait()
            copies[2 * part + 1].wait()
            for start in range(part * span, (part + 1) * span, wide):
                both = mul(k_buf[:, start : start + wide], v_buf[:, start : start + wide], 0, 0)
                middle = start + HEAD_DIM
                out_ref[start:middle] = both[:HEAD_DIM, :HEAD_DIM].astype(BF16)
                out_ref[middle : start + wide] = both[HEAD_DIM:, HEAD_DIM:].astype(BF16)

    return pl.pallas_call(
        kernel,
        in_specs=[IN_PLACE] * 2,
        out_specs=WHOLE,
        out_shape=jax.ShapeDtypeStruct((width, HEAD_DIM), BF16),
        scratch_shapes=[pltpu.VMEM((toks, width), BF16)] * 2
        + [pltpu.SemaphoreType.DMA((2, parts))],
        compiler_params=params(8),
        name="kv_states",
    )(in_hbm(keys), in_hbm(values))


def strict_prefix(pieces, backward):
    count = pieces.shape[0]

    def kernel(x_ref, out_ref):
        total = jnp.zeros(x_ref.shape[1:], F32)
        for step in range(count):
            at = count - 1 - step if backward else step
            out_ref[at] = total.astype(BF16)
            total = total + x_ref[at].astype(F32)

    return pl.pallas_call(
        kernel,
        out_shape=pltpu.HBM(pieces.shape, BF16),
        in_specs=[WHOLE],
        compiler_params=params(4),
        name="strict_prefix",
    )(pieces)


def causal_mask(rows):
    later = lax.broadcasted_iota(jnp.int32, (rows, rows), 0)
    earlier = lax.broadcasted_iota(jnp.int32, (rows, rows), 1)
    return later >= earlier


def head_lanes(head):
    return slice(head * HEAD_DIM, (head + 1) * HEAD_DIM)


def attended_states(queries, keys, values, kv_before, att_scale):
    toks, width = queries.shape
    half = toks // 2

    def kernel(q_ref, k_ref, v_ref, s_ref, out_ref):
        mask = causal_mask(half)
        for head in range(HEADS):
            lanes = head_lanes(head)
            q0, q1 = q_ref[:half, lanes], q_ref[half:, lanes]
            k0, k1 = k_ref[:half, lanes], k_ref[half:, lanes]
            v0, v1 = v_ref[:half, lanes], v_ref[half:, lanes]
            state = s_ref[lanes, :]
            s00 = jnp.where(mask, mul(q0, k0, 1, 1) * att_scale, 0.0).astype(BF16)
            s10 = (mul(q1, k0, 1, 1) * att_scale).astype(BF16)
            s11 = jnp.where(mask, mul(q1, k1, 1, 1) * att_scale, 0.0).astype(BF16)
            out_ref[:half, lanes] = (
                mul(s00, v0, 1, 0) + att_scale * mul(q0, state, 1, 0)
            ).astype(BF16)
            out_ref[half:, lanes] = (
                mul(s10, v0, 1, 0) + mul(s11, v1, 1, 0) + att_scale * mul(q1, state, 1, 0)
            ).astype(BF16)

    return pl.pallas_call(
        kernel,
        in_specs=[WHOLE] * 4,
        out_specs=WHOLE,
        out_shape=jax.ShapeDtypeStruct((toks, width), BF16),
        compiler_params=params(8),
        name="attended",
    )(queries, keys, values, kv_before)


def pair_weight_grad(core, attended, attended_mate, grad, grad_mate, grad_scale):
    toks, width = attended.shape
    half = grad.shape[1] // 2
    rows = 512

    def kernel(core_ref, a_ref, am_ref, g_ref, gm_ref, out_ref, mate_buf, sem):
        features = pl.ds(pl.multiple_of(pl.program_id(0) * rows, rows), rows)
        columns = pl.ds(pl.multiple_of(core_ref[0] * half, half), half)
        copy = pltpu.make_async_copy(gm_ref.at[:, columns], mate_buf, sem)
        first = pl.program_id(0) == 0

        @pl.when(first)
        def _():
            copy.start()

        total = mul(a_ref[:, features], g_ref[:, columns], 0, 0)

        @pl.when(first)
        def _():
            copy.wait()

        total = total + mul(am_ref[:, features], mate_buf[...], 0, 0)
        out_ref[...] = (total * grad_scale).astype(BF16)

    return pl.pallas_call(
        kernel,
        grid=(width // rows,),
        in_specs=[SCALARS] + [WHOLE] * 3 + [IN_PLACE],
        out_specs=pl.BlockSpec((rows, half), lambda i: (i, 0)),
        out_shape=pltpu.HBM((width, half), BF16),
        scratch_shapes=[pltpu.VMEM((toks, half), BF16), pltpu.SemaphoreType.DMA],
        compiler_params=params(14),
        name="pair_weight_grad",
    )(core, attended, attended_mate, grad, in_hbm(grad_mate))


def sum_plane(pieces):
    count, rows, width = pieces.shape
    keep = rows // 2
    slices = width // HEAD_DIM
    parts = 4
    span = width // parts

    def kernel(x_ref, out_ref, buf, sems):
        copies = []
        for part in range(parts):
            lanes = slice(part * span, (part + 1) * span)
            copies.append(
                pltpu.make_async_copy(x_ref.at[:, :, lanes], buf.at[:, :, lanes], sems.at[part])
            )
            copies[part].start()
        for at_slice in range(slices):
            if at_slice % (slices // parts) == 0:
                copies[at_slice // (slices // parts)].wait()
            lanes = head_lanes(at_slice)
            total = buf[0, :, lanes].astype(F32)
            for at in range(1, count):
                total = total + buf[at, :, lanes].astype(F32)
            total = total.astype(BF16)
            out_ref[at_slice, 0] = total[:keep]
            out_ref[at_slice, 1] = total[keep:]

    return pl.pallas_call(
        kernel,
        in_specs=[IN_PLACE],
        out_shape=pltpu.HBM((slices, 2, keep, HEAD_DIM), BF16),
        scratch_shapes=[pltpu.VMEM(pieces.shape, BF16), pltpu.SemaphoreType.DMA((parts,))],
        compiler_params=params(8),
        name="sum_plane",
    )(in_hbm(pieces))


def sum_groups(pieces):
    count = pieces.shape[0]

    def kernel(x_ref, out_ref):
        total = x_ref[0].astype(F32)
        for at in range(1, count):
            total = total + x_ref[at].astype(F32)
        total = total.astype(BF16)
        for at in range(count):
            out_ref[at] = total

    return pl.pallas_call(
        kernel,
        out_shape=pltpu.HBM(pieces.shape, BF16),
        in_specs=[WHOLE],
        out_specs=WHOLE,
        compiler_params=params(4),
        name="sum_groups",
    )(pieces)


def lay_rows(pieces):
    slices, halves, rows, lanes = pieces.shape

    def kernel(x_ref, out_ref):
        for half in range(halves):
            for part in range(slices):
                start = (half * slices + part) * lanes
                out_ref[:, start : start + lanes] = x_ref[part, half].astype(F32)

    return pl.pallas_call(
        kernel,
        out_shape=jax.ShapeDtypeStruct((rows, halves * slices * lanes), F32),
        in_specs=[WHOLE],
        out_specs=WHOLE,
        compiler_params=params(4),
        name="lay_rows",
    )(pieces)


def join_row(places, own, others):
    def kernel(place_ref, own_ref, a_ref, b_ref, c_ref, out_ref):
        x = place_ref[1]
        for by, ref in enumerate((own_ref, a_ref, b_ref, c_ref)):
            out_ref[lax.rem(x - by + 4, 4)] = ref[...]

    return pl.pallas_call(
        kernel,
        in_specs=[SCALARS] + [WHOLE] * 4,
        out_specs=WHOLE,
        out_shape=jax.ShapeDtypeStruct((4, *own.shape), BF16),
        compiler_params=params(4),
        name="join_row",
    )(places, own, *others)


def head_grads(places, grad, queries, attended, mine_parts, mate_parts):
    toks, model = grad.shape
    width = queries.shape[1]
    piece = mine_parts[0].shape[1]
    rows = 8 * piece
    half = width // 2

    def kernel(place_ref, grad_ref, query_ref, a_ref, *refs):
        sides = refs[:4], refs[4:8]
        hg_ref, mine_ref, give_ref, out_ref, g_ref, q_ref, buf, grad_sem, query_sem, sems = refs[8:]
        grad_copy = pltpu.make_async_copy(grad_ref, g_ref, grad_sem)
        grad_copy.start()
        query_copy = pltpu.make_async_copy(query_ref, q_ref, query_sem)
        query_copy.start()
        y, core = place_ref[0], place_ref[2]
        blocks = [lax.rem(y - by + 4, 4) for by in range(4)]
        waits = []
        for by in range(4):
            group = []
            for side in range(2):
                owner = core if side == 0 else 1 - core
                target = buf.at[blocks[by], :, owner]
                group.append(pltpu.make_async_copy(sides[side][by], target, sems.at[by, side]))
            waits.append(group)
        order = (0, 1, 3, 2)
        for by in order:
            for copy in waits[by]:
                copy.start()
        grad_copy.wait()
        query_copy.wait()
        for by in order:
            for copy in waits[by]:
                copy.wait()
            lanes = pl.ds(pl.multiple_of(blocks[by] * rows, rows), rows)
            block = buf[blocks[by]].reshape(rows, model)
            middle = toks // 2
            head_grad = jnp.concatenate(
                [mul(g_ref[:middle], block, 1, 1), mul(g_ref[middle:], block, 1, 1)], 0
            ).astype(BF16)
            hg_ref[:, lanes] = head_grad
            query = q_ref[:, lanes]
            states = [
                mul(query[:, head_lanes(h)], head_grad[:, head_lanes(h)], 0, 0)
                for h in range(rows // HEAD_DIM)
            ]
            state = jnp.concatenate(states, 0).astype(BF16)
            place = pl.ds(pl.multiple_of(lax.rem(blocks[by], 2) * rows, rows), rows)
            here = blocks[by] // 2 == core

            @pl.when(here)
            def _():
                mine_ref[place, :] = state

            @pl.when(jnp.logical_not(here))
            def _():
                give_ref[place, :] = state

        for start in range(0, model, 512):
            columns = slice(start, start + 512)
            wide = buf[:, :, :, :, columns].reshape(width, 512)
            out_ref[:, columns] = mul(a_ref[...], wide, 1, 0).astype(BF16)

    return pl.pallas_call(
        kernel,
        in_specs=[SCALARS, IN_PLACE, IN_PLACE, WHOLE] + [IN_PLACE] * 8,
        out_specs=[WHOLE] * 4,
        out_shape=[
            jax.ShapeDtypeStruct((toks, width), BF16),
            jax.ShapeDtypeStruct((half, HEAD_DIM), BF16),
            jax.ShapeDtypeStruct((half, HEAD_DIM), BF16),
            jax.ShapeDtypeStruct((toks, model), BF16),
        ],
        scratch_shapes=[
            pltpu.VMEM((toks, model), BF16),
            pltpu.VMEM((toks, width), BF16),
            pltpu.VMEM((4, 4, 2, piece, model), BF16),
            pltpu.SemaphoreType.DMA,
            pltpu.SemaphoreType.DMA,
            pltpu.SemaphoreType.DMA((4, 2)),
        ],
        compiler_params=params(12),
        name="head_grads",
    )(places, in_hbm(grad), in_hbm(queries), attended, *[in_hbm(part) for part in (*mine_parts, *mate_parts)])


def chip_states(mine, mate):
    def kernel(a_ref, b_ref, out_ref):
        out_ref[...] = (a_ref[...].astype(F32) + b_ref[...].astype(F32)).astype(BF16)

    return pl.pallas_call(
        kernel,
        in_specs=[WHOLE] * 2,
        out_specs=WHOLE,
        out_shape=jax.ShapeDtypeStruct(mine.shape, BF16),
        compiler_params=params(4),
        name="chip_states",
    )(mine, mate)


def row_states(places, chip, pieces):
    def kernel(place_ref, chip_ref, a_ref, b_ref, c_ref, row_ref, later_ref):
        x = place_ref[1]
        total, later = chip_ref[...].astype(F32), jnp.zeros(chip_ref.shape, F32)
        for by, ref in enumerate((a_ref, b_ref, c_ref), 1):
            piece = ref[...].astype(F32)
            total = total + piece
            later = later + jnp.where(x + by < 4, piece, 0.0)
        row_ref[...] = total.astype(BF16)
        later_ref[...] = later

    return pl.pallas_call(
        kernel,
        in_specs=[pl.BlockSpec(memory_space=pltpu.SMEM)] + [WHOLE] * 4,
        out_specs=[WHOLE] * 2,
        out_shape=[jax.ShapeDtypeStruct(chip.shape, BF16), jax.ShapeDtypeStruct(chip.shape, F32)],
        compiler_params=params(4),
        name="row_states",
    )(places, chip, *pieces)


def final_states(places, later_here, mine, mate, pieces):
    def kernel(place_ref, later_ref, mine_ref, mate_ref, a_ref, b_ref, c_ref, keep_ref, give_ref):
        y, core = place_ref[0], place_ref[2]
        later = later_ref[...]
        for by, ref in enumerate((a_ref, b_ref, c_ref), 1):
            later = later + jnp.where(y + by < 4, ref[...].astype(F32), 0.0)
        second = jnp.where(core == 0, mate_ref[...], mine_ref[...]).astype(F32)
        first_core, second_core = later + second, later
        keep_ref[...] = jnp.where(core == 0, first_core, second_core).astype(BF16)
        give_ref[...] = jnp.where(core == 0, second_core, first_core).astype(BF16)

    return pl.pallas_call(
        kernel,
        in_specs=[pl.BlockSpec(memory_space=pltpu.SMEM)] + [WHOLE] * 6,
        out_specs=[WHOLE] * 2,
        out_shape=[jax.ShapeDtypeStruct(mine.shape, BF16)] * 2,
        compiler_params=params(4),
        name="final_states",
    )(places, later_here, mine, mate, *pieces)


def local_grads(queries, keys, values, head_grad, kv_before, att_scale):
    toks, width = queries.shape
    half = toks // 2
    group = HEADS // 2

    def kernel(q_ref, k_ref, v_ref, g_ref, kv_ref, dq_ref, dk_ref, dv_ref):
        positions = lax.broadcasted_iota(jnp.int32, (half, half), 0)
        sources = lax.broadcasted_iota(jnp.int32, (half, half), 1)
        causal, turned = positions >= sources, positions <= sources

        def scaled(left, right, mask=None):
            scores = mul(left, right, 1, 1) * att_scale
            return (scores if mask is None else jnp.where(mask, scores, 0.0)).astype(BF16)

        for head in range(group):
            first = (pl.program_id(0) * group + head) * HEAD_DIM
            lanes = pl.ds(pl.multiple_of(first, HEAD_DIM), HEAD_DIM)
            here = head_lanes(head)
            q0, q1 = q_ref[:half, lanes], q_ref[half:, lanes]
            k0, k1 = k_ref[:half, lanes], k_ref[half:, lanes]
            v0, v1 = v_ref[:half, lanes], v_ref[half:, lanes]
            g0, g1 = g_ref[:half, lanes], g_ref[half:, lanes]
            kv = kv_ref[lanes, :]
            dv_ref[:half, here] = mul(scaled(k0, q0, turned), g0, 1, 0) + mul(
                scaled(k0, q1), g1, 1, 0
            )
            dv_ref[half:, here] = mul(scaled(k1, q1, turned), g1, 1, 0)
            b00, b10, b11 = scaled(g0, v0, causal), scaled(g1, v0), scaled(g1, v1, causal)
            dk_ref[:half, here] = mul(b00, q0, 0, 0) + mul(b10, q1, 0, 0)
            dk_ref[half:, here] = mul(b11, q1, 0, 0)
            dq_ref[:half, here] = (mul(b00, k0, 1, 0) + att_scale * mul(g0, kv, 1, 1)).astype(BF16)
            dq_ref[half:, here] = (
                mul(b10, k0, 1, 0) + mul(b11, k1, 1, 0) + att_scale * mul(g1, kv, 1, 1)
            ).astype(BF16)

    return pl.pallas_call(
        kernel,
        grid=(HEADS // group,),
        in_specs=[WHOLE] * 5,
        out_specs=[pl.BlockSpec((toks, group * HEAD_DIM), lambda i: (0, i))] * 3,
        out_shape=[
            pltpu.HBM((toks, width), BF16),
            pltpu.HBM((toks, width), F32),
            pltpu.HBM((toks, width), F32),
        ],
        compiler_params=params(12),
        name="local_grads",
    )(queries, keys, values, head_grad, kv_before)


def later_grads(core, keys, values, key_local, value_local, keep, back, att_scale):
    toks, width = keys.shape
    heads = keep.shape[0] // HEAD_DIM
    rows = 256

    def kernel(core_ref, k_ref, v_ref, dkl_ref, dvl_ref, keep_ref, back_ref, dk_ref, dv_ref):
        here = pl.ds(pl.multiple_of(pl.program_id(0) * rows, rows), rows)
        for head in range(HEADS):
            lanes, state = head_lanes(head), head_lanes(head % heads)
            mine = core_ref[0] == head // heads
            qg = jnp.where(mine, keep_ref[state, :], back_ref[state, :])
            dk_ref[:, lanes] = (
                dkl_ref[:, lanes] + att_scale * mul(v_ref[here, lanes], qg, 1, 1)
            ).astype(BF16)
            dv_ref[:, lanes] = (
                dvl_ref[:, lanes] + att_scale * mul(k_ref[here, lanes], qg, 1, 0)
            ).astype(BF16)

    block = pl.BlockSpec((rows, width), lambda i: (i, 0))
    return pl.pallas_call(
        kernel,
        grid=(toks // rows,),
        in_specs=[SCALARS, WHOLE, WHOLE, block, block, WHOLE, WHOLE],
        out_specs=[block] * 2,
        out_shape=[pltpu.HBM((toks, width), BF16)] * 2,
        compiler_params=params(8),
        name="later_grads",
    )(core, keys, values, in_hbm(key_local), in_hbm(value_local), keep, back)


def swap_cores(value):
    return lax.ppermute(value, "core", [(0, 1), (1, 0)])


def turn(value, axis, count, by):
    return lax.ppermute(value, axis, [(at, (at + by) % count) for at in range(count)])


def after(value, *others):
    return lax.optimization_barrier((value,) + others)[0]


def around(value, axis, sign):
    return [turn(value, axis, 4, sign * by) for by in (1, 2, 3)]


def on_device(query_in, key_in, value_in, out_grad, out_weight):
    queries, keys, values, grad = query_in[0], key_in[0], value_in[0], out_grad[0]
    toks = queries.shape[0]
    length = toks * 32
    att_scale = 1.0 / math.sqrt(HEAD_DIM * length)
    grad_scale = 1.0 / math.sqrt(length * 8)
    core = lax.axis_index("core")
    half = grad.shape[1] // 2
    places = jnp.stack([lax.axis_index("y"), lax.axis_index("x"), core])
    core_place = jnp.reshape(core, (1,))

    shards = around(out_weight, "x", 1)
    far_shard = turn(out_weight, "y", 4, 2)
    grad_mate = swap_cores(grad)
    kv_block = kv_states(keys, values)

    pieces = lax.all_to_all(kv_block.reshape(32, -1, HEAD_DIM), CONTEXT, 0, 0)
    prefixes = strict_prefix(after(pieces, grad_mate, far_shard, *shards), False)
    row = join_row(places, after(out_weight, prefixes), shards)
    low, high = turn(row, "y", 4, 1), turn(row, "y", 4, -1)
    far_shard = after(far_shard, prefixes)
    far_shards = around(far_shard, "x", 1)
    kv_before = lax.all_to_all(prefixes, CONTEXT, 0, 0).reshape(kv_block.shape)

    far_row = join_row(places, far_shard, far_shards)
    row_mate = swap_cores(row)
    kv_before = after(kv_before, low, high, far_row, row_mate)
    attended = attended_states(queries, keys, values, kv_before, att_scale)
    attended_mate = swap_cores(attended)
    terms = pair_weight_grad(core_place, attended, attended_mate, grad, grad_mate, grad_scale)
    plane_terms = lax.all_to_all(terms.reshape(16, 64, half), PLANE, 0, 0)

    weight_mine = [row, low, far_row, high]
    weight_mate = [row_mate] + [swap_cores(after(part, terms)) for part in weight_mine[1:]]
    head_grad, mine, give, output = head_grads(
        after(places, terms), grad, queries, attended, weight_mine, weight_mate
    )
    mate = swap_cores(give)
    chip = chip_states(mine, mate)
    chip_pieces = around(chip, "x", -1)
    query_grad, key_local, value_local = local_grads(
        queries, keys, values, head_grad, kv_before, att_scale
    )

    plane_sum = sum_plane(after(plane_terms, key_local))
    chip_pieces = [after(piece, plane_sum) for piece in chip_pieces]
    row_state, later_here = row_states(places, chip, chip_pieces)
    plane_sum = after(plane_sum, row_state)
    group_terms = lax.all_to_all(plane_sum.reshape(16, 32, HEAD_DIM), ("z", "core"), 0, 0)
    row_pieces = around(after(row_state, plane_sum), "y", -1)
    keep, give = final_states(places, later_here, mine, mate, row_pieces)
    back = swap_cores(give)
    group_sum = sum_groups(group_terms.reshape(8, 2, 32, HEAD_DIM))
    weight_grad = lay_rows(lax.all_to_all(group_sum, "z", 0, 0))

    key_grad, value_grad = later_grads(
        core_place, keys, values, key_local, value_local, after(keep, group_sum), back, att_scale
    )
    return (output[None], query_grad[None], key_grad[None], value_grad[None], weight_grad)


def solution(mesh):
    fine = Mesh(mesh.devices.reshape(8, 4, 4, 2), ("z", "y", "x", "core"))
    rows = P("z", CONTEXT, None)
    owned = P(CONTEXT, None)
    return jax.shard_map(
        on_device,
        mesh=fine,
        in_specs=(rows, rows, rows, rows, owned),
        out_specs=(rows, rows, rows, rows, owned),
        check_vma=False,
    )
```

```python
import math

import jax
import jax.numpy as jnp
from jax import lax
from jax.experimental import pallas as pl
from jax.experimental.pallas import tpu as pltpu
from jax.sharding import Mesh
from jax.sharding import PartitionSpec as P

HEADS = 8
HEAD_DIM = 128
BF16 = jnp.bfloat16
F32 = jnp.float32
CONTEXT = ("y", "x", "core")
PLANE = ("y", "x")
WHOLE = pl.BlockSpec(memory_space=pltpu.VMEM)
SCALARS = pl.BlockSpec(memory_space=pltpu.SMEM)
IN_PLACE = pl.BlockSpec(memory_space=pl.ANY)


def params(mib=16):
    return pltpu.CompilerParams(vmem_limit_bytes=mib * 1024 * 1024)


def in_hbm(value):
    return pltpu.with_memory_space_constraint(value, pltpu.HBM)


def mul(a, b, a_dim, b_dim):
    return lax.dot_general(
        a, b, (((a_dim,), (b_dim,)), ((), ())), preferred_element_type=F32
    )


def kv_states(keys, values):
    toks, width = keys.shape
    wide = 2 * HEAD_DIM
    parts = 2
    span = width // parts

    def kernel(k_ref, v_ref, out_ref, k_buf, v_buf, sems):
        copies = []
        for part in range(parts):
            lanes = slice(part * span, (part + 1) * span)
            for at, (src, dst) in enumerate(((k_ref, k_buf), (v_ref, v_buf))):
                copy = pltpu.make_async_copy(src.at[:, lanes], dst.at[:, lanes], sems.at[at, part])
                copy.start()
                copies.append(copy)
        for part in range(parts):
            copies[2 * part].wait()
            copies[2 * part + 1].wait()
            for start in range(part * span, (part + 1) * span, wide):
                both = mul(k_buf[:, start : start + wide], v_buf[:, start : start + wide], 0, 0)
                middle = start + HEAD_DIM
                out_ref[start:middle] = both[:HEAD_DIM, :HEAD_DIM].astype(BF16)
                out_ref[middle : start + wide] = both[HEAD_DIM:, HEAD_DIM:].astype(BF16)

    return pl.pallas_call(
        kernel,
        in_specs=[IN_PLACE] * 2,
        out_specs=WHOLE,
        out_shape=jax.ShapeDtypeStruct((width, HEAD_DIM), BF16),
        scratch_shapes=[pltpu.VMEM((toks, width), BF16)] * 2
        + [pltpu.SemaphoreType.DMA((2, parts))],
        compiler_params=params(8),
        name="kv_states",
    )(in_hbm(keys), in_hbm(values))


def strict_prefix(pieces, backward):
    count = pieces.shape[0]

    def kernel(x_ref, out_ref):
        total = jnp.zeros(x_ref.shape[1:], F32)
        for step in range(count):
            at = count - 1 - step if backward else step
            out_ref[at] = total.astype(BF16)
            total = total + x_ref[at].astype(F32)

    return pl.pallas_call(
        kernel,
        out_shape=pltpu.HBM(pieces.shape, BF16),
        in_specs=[WHOLE],
        compiler_params=params(4),
        name="strict_prefix",
    )(pieces)


def causal_mask(rows):
    later = lax.broadcasted_iota(jnp.int32, (rows, rows), 0)
    earlier = lax.broadcasted_iota(jnp.int32, (rows, rows), 1)
    return later >= earlier


def head_lanes(head):
    return slice(head * HEAD_DIM, (head + 1) * HEAD_DIM)


def attended_states(queries, keys, values, kv_before, att_scale):
    toks, width = queries.shape
    half = toks // 2

    def kernel(q_ref, k_ref, v_ref, s_ref, out_ref):
        mask = causal_mask(half)
        for head in range(HEADS):
            lanes = head_lanes(head)
            q0, q1 = q_ref[:half, lanes], q_ref[half:, lanes]
            k0, k1 = k_ref[:half, lanes], k_ref[half:, lanes]
            v0, v1 = v_ref[:half, lanes], v_ref[half:, lanes]
            state = s_ref[lanes, :]
            s00 = jnp.where(mask, mul(q0, k0, 1, 1) * att_scale, 0.0).astype(BF16)
            s10 = (mul(q1, k0, 1, 1) * att_scale).astype(BF16)
            s11 = jnp.where(mask, mul(q1, k1, 1, 1) * att_scale, 0.0).astype(BF16)
            out_ref[:half, lanes] = (
                mul(s00, v0, 1, 0) + att_scale * mul(q0, state, 1, 0)
            ).astype(BF16)
            out_ref[half:, lanes] = (
                mul(s10, v0, 1, 0) + mul(s11, v1, 1, 0) + att_scale * mul(q1, state, 1, 0)
            ).astype(BF16)

    return pl.pallas_call(
        kernel,
        in_specs=[WHOLE] * 4,
        out_specs=WHOLE,
        out_shape=jax.ShapeDtypeStruct((toks, width), BF16),
        compiler_params=params(8),
        name="attended",
    )(queries, keys, values, kv_before)


def pair_weight_grad(core, attended, attended_mate, grad, grad_mate, grad_scale):
    toks, width = attended.shape
    half = grad.shape[1] // 2
    rows = 512

    def kernel(core_ref, a_ref, am_ref, g_ref, gm_ref, out_ref, mate_buf, sem):
        features = pl.ds(pl.multiple_of(pl.program_id(0) * rows, rows), rows)
        columns = pl.ds(pl.multiple_of(core_ref[0] * half, half), half)
        copy = pltpu.make_async_copy(gm_ref.at[:, columns], mate_buf, sem)
        first = pl.program_id(0) == 0

        @pl.when(first)
        def _():
            copy.start()

        total = mul(a_ref[:, features], g_ref[:, columns], 0, 0)

        @pl.when(first)
        def _():
            copy.wait()

        total = total + mul(am_ref[:, features], mate_buf[...], 0, 0)
        out_ref[...] = (total * grad_scale).astype(BF16)

    return pl.pallas_call(
        kernel,
        grid=(width // rows,),
        in_specs=[SCALARS] + [WHOLE] * 3 + [IN_PLACE],
        out_specs=pl.BlockSpec((rows, half), lambda i: (i, 0)),
        out_shape=pltpu.HBM((width, half), BF16),
        scratch_shapes=[pltpu.VMEM((toks, half), BF16), pltpu.SemaphoreType.DMA],
        compiler_params=params(14),
        name="pair_weight_grad",
    )(core, attended, attended_mate, grad, in_hbm(grad_mate))


def sum_plane(pieces):
    count, rows, width = pieces.shape
    keep = rows // 2
    slices = width // HEAD_DIM
    parts = 8
    span = width // parts

    def kernel(x_ref, out_ref, buf, sems):
        copies = []
        for part in range(parts):
            lanes = slice(part * span, (part + 1) * span)
            copies.append(
                pltpu.make_async_copy(x_ref.at[:, :, lanes], buf.at[:, :, lanes], sems.at[part])
            )
            copies[part].start()
        for at_slice in range(slices):
            if at_slice % (slices // parts) == 0:
                copies[at_slice // (slices // parts)].wait()
            lanes = head_lanes(at_slice)
            total = buf[0, :, lanes].astype(F32)
            for at in range(1, count):
                total = total + buf[at, :, lanes].astype(F32)
            total = total.astype(BF16)
            out_ref[at_slice, 0] = total[:keep]
            out_ref[at_slice, 1] = total[keep:]

    return pl.pallas_call(
        kernel,
        in_specs=[IN_PLACE],
        out_shape=pltpu.HBM((slices, 2, keep, HEAD_DIM), BF16),
        scratch_shapes=[pltpu.VMEM(pieces.shape, BF16), pltpu.SemaphoreType.DMA((parts,))],
        compiler_params=params(8),
        name="sum_plane",
    )(in_hbm(pieces))


def sum_groups(pieces):
    count = pieces.shape[0]

    def kernel(x_ref, out_ref):
        total = x_ref[0].astype(F32)
        for at in range(1, count):
            total = total + x_ref[at].astype(F32)
        total = total.astype(BF16)
        for at in range(count):
            out_ref[at] = total

    return pl.pallas_call(
        kernel,
        out_shape=pltpu.HBM(pieces.shape, BF16),
        in_specs=[WHOLE],
        out_specs=WHOLE,
        compiler_params=params(4),
        name="sum_groups",
    )(pieces)


def lay_rows(pieces):
    slices, halves, rows, lanes = pieces.shape

    def kernel(x_ref, out_ref):
        for half in range(halves):
            for part in range(slices):
                start = (half * slices + part) * lanes
                out_ref[:, start : start + lanes] = x_ref[part, half].astype(F32)

    return pl.pallas_call(
        kernel,
        out_shape=jax.ShapeDtypeStruct((rows, halves * slices * lanes), F32),
        in_specs=[WHOLE],
        out_specs=WHOLE,
        compiler_params=params(4),
        name="lay_rows",
    )(pieces)


def join_row(places, own, others):
    def kernel(place_ref, own_ref, a_ref, b_ref, c_ref, out_ref):
        x = place_ref[1]
        for by, ref in enumerate((own_ref, a_ref, b_ref, c_ref)):
            out_ref[lax.rem(x - by + 4, 4)] = ref[...]

    return pl.pallas_call(
        kernel,
        in_specs=[SCALARS] + [WHOLE] * 4,
        out_specs=WHOLE,
        out_shape=jax.ShapeDtypeStruct((4, *own.shape), BF16),
        compiler_params=params(4),
        name="join_row",
    )(places, own, *others)


def head_grads(places, grad, queries, attended, mine_parts, mate_parts):
    toks, model = grad.shape
    width = queries.shape[1]
    piece = mine_parts[0].shape[1]
    rows = 8 * piece
    half = width // 2

    def kernel(place_ref, grad_ref, query_ref, a_ref, *refs):
        sides = refs[:4], refs[4:8]
        hg_ref, mine_ref, give_ref, out_ref, g_ref, q_ref, buf, grad_sem, query_sem, sems = refs[8:]
        grad_copy = pltpu.make_async_copy(grad_ref, g_ref, grad_sem)
        grad_copy.start()
        query_copy = pltpu.make_async_copy(query_ref, q_ref, query_sem)
        query_copy.start()
        y, core = place_ref[0], place_ref[2]
        blocks = [lax.rem(y - by + 4, 4) for by in range(4)]
        waits = []
        for by in range(4):
            group = []
            for side in range(2):
                owner = core if side == 0 else 1 - core
                target = buf.at[blocks[by], :, owner]
                group.append(pltpu.make_async_copy(sides[side][by], target, sems.at[by, side]))
            waits.append(group)
        order = (0, 1, 3, 2)
        for by in order:
            for copy in waits[by]:
                copy.start()
        grad_copy.wait()
        query_copy.wait()
        for by in order:
            for copy in waits[by]:
                copy.wait()
            lanes = pl.ds(pl.multiple_of(blocks[by] * rows, rows), rows)
            block = buf[blocks[by]].reshape(rows, model)
            middle = toks // 2
            head_grad = jnp.concatenate(
                [mul(g_ref[:middle], block, 1, 1), mul(g_ref[middle:], block, 1, 1)], 0
            ).astype(BF16)
            hg_ref[:, lanes] = head_grad
            query = q_ref[:, lanes]
            states = [
                mul(query[:, head_lanes(h)], head_grad[:, head_lanes(h)], 0, 0)
                for h in range(rows // HEAD_DIM)
            ]
            state = jnp.concatenate(states, 0).astype(BF16)
            place = pl.ds(pl.multiple_of(lax.rem(blocks[by], 2) * rows, rows), rows)
            here = blocks[by] // 2 == core

            @pl.when(here)
            def _():
                mine_ref[place, :] = state

            @pl.when(jnp.logical_not(here))
            def _():
                give_ref[place, :] = state

        for start in range(0, model, 512):
            columns = slice(start, start + 512)
            wide = buf[:, :, :, :, columns].reshape(width, 512)
            out_ref[:, columns] = mul(a_ref[...], wide, 1, 0).astype(BF16)

    return pl.pallas_call(
        kernel,
        in_specs=[SCALARS, IN_PLACE, IN_PLACE, WHOLE] + [IN_PLACE] * 8,
        out_specs=[WHOLE] * 4,
        out_shape=[
            jax.ShapeDtypeStruct((toks, width), BF16),
            jax.ShapeDtypeStruct((half, HEAD_DIM), BF16),
            jax.ShapeDtypeStruct((half, HEAD_DIM), BF16),
            jax.ShapeDtypeStruct((toks, model), BF16),
        ],
        scratch_shapes=[
            pltpu.VMEM((toks, model), BF16),
            pltpu.VMEM((toks, width), BF16),
            pltpu.VMEM((4, 4, 2, piece, model), BF16),
            pltpu.SemaphoreType.DMA,
            pltpu.SemaphoreType.DMA,
            pltpu.SemaphoreType.DMA((4, 2)),
        ],
        compiler_params=params(12),
        name="head_grads",
    )(places, in_hbm(grad), in_hbm(queries), attended, *[in_hbm(part) for part in (*mine_parts, *mate_parts)])


def chip_states(mine, mate):
    def kernel(a_ref, b_ref, out_ref):
        out_ref[...] = (a_ref[...].astype(F32) + b_ref[...].astype(F32)).astype(BF16)

    return pl.pallas_call(
        kernel,
        in_specs=[WHOLE] * 2,
        out_specs=WHOLE,
        out_shape=jax.ShapeDtypeStruct(mine.shape, BF16),
        compiler_params=params(4),
        name="chip_states",
    )(mine, mate)


def row_states(places, chip, pieces):
    def kernel(place_ref, chip_ref, a_ref, b_ref, c_ref, row_ref, later_ref):
        x = place_ref[1]
        total, later = chip_ref[...].astype(F32), jnp.zeros(chip_ref.shape, F32)
        for by, ref in enumerate((a_ref, b_ref, c_ref), 1):
            piece = ref[...].astype(F32)
            total = total + piece
            later = later + jnp.where(x + by < 4, piece, 0.0)
        row_ref[...] = total.astype(BF16)
        later_ref[...] = later

    return pl.pallas_call(
        kernel,
        in_specs=[pl.BlockSpec(memory_space=pltpu.SMEM)] + [WHOLE] * 4,
        out_specs=[WHOLE] * 2,
        out_shape=[jax.ShapeDtypeStruct(chip.shape, BF16), jax.ShapeDtypeStruct(chip.shape, F32)],
        compiler_params=params(4),
        name="row_states",
    )(places, chip, *pieces)


def final_states(places, later_here, mine, mate, pieces):
    def kernel(place_ref, later_ref, mine_ref, mate_ref, a_ref, b_ref, c_ref, keep_ref, give_ref):
        y, core = place_ref[0], place_ref[2]
        later = later_ref[...]
        for by, ref in enumerate((a_ref, b_ref, c_ref), 1):
            later = later + jnp.where(y + by < 4, ref[...].astype(F32), 0.0)
        second = jnp.where(core == 0, mate_ref[...], mine_ref[...]).astype(F32)
        first_core, second_core = later + second, later
        keep_ref[...] = jnp.where(core == 0, first_core, second_core).astype(BF16)
        give_ref[...] = jnp.where(core == 0, second_core, first_core).astype(BF16)

    return pl.pallas_call(
        kernel,
        in_specs=[pl.BlockSpec(memory_space=pltpu.SMEM)] + [WHOLE] * 6,
        out_specs=[WHOLE] * 2,
        out_shape=[jax.ShapeDtypeStruct(mine.shape, BF16)] * 2,
        compiler_params=params(4),
        name="final_states",
    )(places, later_here, mine, mate, *pieces)


def local_grads(queries, keys, values, head_grad, kv_before, att_scale):
    toks, width = queries.shape
    half = toks // 2
    group = HEADS // 2

    def kernel(q_ref, k_ref, v_ref, g_ref, kv_ref, dq_ref, dk_ref, dv_ref):
        positions = lax.broadcasted_iota(jnp.int32, (half, half), 0)
        sources = lax.broadcasted_iota(jnp.int32, (half, half), 1)
        causal, turned = positions >= sources, positions <= sources

        def scaled(left, right, mask=None):
            scores = mul(left, right, 1, 1) * att_scale
            return (scores if mask is None else jnp.where(mask, scores, 0.0)).astype(BF16)

        for head in range(group):
            first = (pl.program_id(0) * group + head) * HEAD_DIM
            lanes = pl.ds(pl.multiple_of(first, HEAD_DIM), HEAD_DIM)
            here = head_lanes(head)
            q0, q1 = q_ref[:half, lanes], q_ref[half:, lanes]
            k0, k1 = k_ref[:half, lanes], k_ref[half:, lanes]
            v0, v1 = v_ref[:half, lanes], v_ref[half:, lanes]
            g0, g1 = g_ref[:half, lanes], g_ref[half:, lanes]
            kv = kv_ref[lanes, :]
            dv_ref[:half, here] = mul(scaled(k0, q0, turned), g0, 1, 0) + mul(
                scaled(k0, q1), g1, 1, 0
            )
            dv_ref[half:, here] = mul(scaled(k1, q1, turned), g1, 1, 0)
            b00, b10, b11 = scaled(g0, v0, causal), scaled(g1, v0), scaled(g1, v1, causal)
            dk_ref[:half, here] = mul(b00, q0, 0, 0) + mul(b10, q1, 0, 0)
            dk_ref[half:, here] = mul(b11, q1, 0, 0)
            dq_ref[:half, here] = (mul(b00, k0, 1, 0) + att_scale * mul(g0, kv, 1, 1)).astype(BF16)
            dq_ref[half:, here] = (
                mul(b10, k0, 1, 0) + mul(b11, k1, 1, 0) + att_scale * mul(g1, kv, 1, 1)
            ).astype(BF16)

    return pl.pallas_call(
        kernel,
        grid=(HEADS // group,),
        in_specs=[WHOLE] * 5,
        out_specs=[pl.BlockSpec((toks, group * HEAD_DIM), lambda i: (0, i))] * 3,
        out_shape=[
            pltpu.HBM((toks, width), BF16),
            pltpu.HBM((toks, width), F32),
            pltpu.HBM((toks, width), F32),
        ],
        compiler_params=params(12),
        name="local_grads",
    )(queries, keys, values, head_grad, kv_before)


def later_grads(core, keys, values, key_local, value_local, keep, back, att_scale):
    toks, width = keys.shape
    heads = keep.shape[0] // HEAD_DIM
    rows = 256

    def kernel(core_ref, k_ref, v_ref, dkl_ref, dvl_ref, keep_ref, back_ref, dk_ref, dv_ref):
        here = pl.ds(pl.multiple_of(pl.program_id(0) * rows, rows), rows)
        for head in range(HEADS):
            lanes, state = head_lanes(head), head_lanes(head % heads)
            mine = core_ref[0] == head // heads
            qg = jnp.where(mine, keep_ref[state, :], back_ref[state, :])
            dk_ref[:, lanes] = (
                dkl_ref[:, lanes] + att_scale * mul(v_ref[here, lanes], qg, 1, 1)
            ).astype(BF16)
            dv_ref[:, lanes] = (
                dvl_ref[:, lanes] + att_scale * mul(k_ref[here, lanes], qg, 1, 0)
            ).astype(BF16)

    block = pl.BlockSpec((rows, width), lambda i: (i, 0))
    return pl.pallas_call(
        kernel,
        grid=(toks // rows,),
        in_specs=[SCALARS, WHOLE, WHOLE, block, block, WHOLE, WHOLE],
        out_specs=[block] * 2,
        out_shape=[pltpu.HBM((toks, width), BF16)] * 2,
        compiler_params=params(8),
        name="later_grads",
    )(core, keys, values, in_hbm(key_local), in_hbm(value_local), keep, back)


def swap_cores(value):
    return lax.ppermute(value, "core", [(0, 1), (1, 0)])


def turn(value, axis, count, by):
    return lax.ppermute(value, axis, [(at, (at + by) % count) for at in range(count)])


def after(value, *others):
    return lax.optimization_barrier((value,) + others)[0]


def around(value, axis, sign):
    return [turn(value, axis, 4, sign * by) for by in (1, 2, 3)]


def on_device(query_in, key_in, value_in, out_grad, out_weight):
    queries, keys, values, grad = query_in[0], key_in[0], value_in[0], out_grad[0]
    toks = queries.shape[0]
    length = toks * 32
    att_scale = 1.0 / math.sqrt(HEAD_DIM * length)
    grad_scale = 1.0 / math.sqrt(length * 8)
    core = lax.axis_index("core")
    half = grad.shape[1] // 2
    places = jnp.stack([lax.axis_index("y"), lax.axis_index("x"), core])
    core_place = jnp.reshape(core, (1,))

    shards = around(out_weight, "x", 1)
    far_shard = turn(out_weight, "y", 4, 2)
    grad_mate = swap_cores(grad)
    kv_block = kv_states(keys, values)

    pieces = lax.all_to_all(kv_block.reshape(32, -1, HEAD_DIM), CONTEXT, 0, 0)
    prefixes = strict_prefix(after(pieces, grad_mate, far_shard, *shards), False)
    row = join_row(places, after(out_weight, prefixes), shards)
    low, high = turn(row, "y", 4, 1), turn(row, "y", 4, -1)
    far_shard = after(far_shard, prefixes)
    far_shards = around(far_shard, "x", 1)
    kv_before = lax.all_to_all(prefixes, CONTEXT, 0, 0).reshape(kv_block.shape)

    far_row = join_row(places, far_shard, far_shards)
    row_mate = swap_cores(row)
    kv_before = after(kv_before, low, high, far_row, row_mate)
    attended = attended_states(queries, keys, values, kv_before, att_scale)
    attended_mate = swap_cores(attended)
    terms = pair_weight_grad(core_place, attended, attended_mate, grad, grad_mate, grad_scale)
    plane_terms = lax.all_to_all(terms.reshape(16, 64, half), PLANE, 0, 0)

    weight_mine = [row, low, far_row, high]
    weight_mate = [row_mate] + [swap_cores(after(part, terms)) for part in weight_mine[1:]]
    head_grad, mine, give, output = head_grads(
        after(places, terms), grad, queries, attended, weight_mine, weight_mate
    )
    mate = swap_cores(give)
    chip = chip_states(mine, mate)
    chip_pieces = around(chip, "x", -1)
    query_grad, key_local, value_local = local_grads(
        queries, keys, values, head_grad, kv_before, att_scale
    )

    plane_sum = sum_plane(after(plane_terms, key_local))
    chip_pieces = [after(piece, plane_sum) for piece in chip_pieces]
    row_state, later_here = row_states(places, chip, chip_pieces)
    plane_sum = after(plane_sum, row_state)
    group_terms = lax.all_to_all(plane_sum.reshape(16, 32, HEAD_DIM), ("z", "core"), 0, 0)
    row_pieces = around(after(row_state, plane_sum), "y", -1)
    keep, give = final_states(places, later_here, mine, mate, row_pieces)
    back = swap_cores(give)
    group_sum = sum_groups(group_terms.reshape(8, 2, 32, HEAD_DIM))
    weight_grad = lay_rows(lax.all_to_all(group_sum, "z", 0, 0))

    key_grad, value_grad = later_grads(
        core_place, keys, values, key_local, value_local, after(keep, group_sum), back, att_scale
    )
    return (output[None], query_grad[None], key_grad[None], value_grad[None], weight_grad)


def solution(mesh):
    fine = Mesh(mesh.devices.reshape(8, 4, 4, 2), ("z", "y", "x", "core"))
    rows = P("z", CONTEXT, None)
    owned = P(CONTEXT, None)
    return jax.shard_map(
        on_device,
        mesh=fine,
        in_specs=(rows, rows, rows, rows, owned),
        out_specs=(rows, rows, rows, rows, owned),
        check_vma=False,
    )
```
